256 devices in a mesh: pipe: 4 (over y_hi, core), ctx: 16 (over y_lo, z), tp: 4 (over x).
Axes of the slice: x: 4, y: 4 (y_hi: 2, y_lo: 2; y = y_hi * 2 + y_lo), z: 8, core: 2. Of those that a mesh axis runs over, the one named last changes fastest.
Arguments:
- query_rows: bfloat16 [8192, 64, 128], P(('pipe', 'ctx'), 'tp'), may hold values from -100 to 100
- key_rows: bfloat16 [8192, 4, 128], P(('pipe', 'ctx'), 'tp'), may hold values from -6 to 6
- value_rows: bfloat16 [8192, 4, 128], P(('pipe', 'ctx'), 'tp'), may hold values from -6 to 6
- doc_ids: int32 [8192], P(('pipe', 'ctx')), may hold values from 0 to 3, never falling along the last dimension, each value on 1 to 4096 neighbouring positions
- out_weight: bfloat16 [8192, 8192], P('tp', 'ctx'), may hold values from -0.25 to 0.25
Outputs:
- projected: bfloat16 [4, 16, 4, 32, 8192], P('pipe', None, 'tp', None, 'ctx')
The draws below stay inside these ranges and needn't reach their ends.
Inputs may be any that keep to these rules, and one draw needn't show every extreme that they name: `doc_ids`: ids never fall along the book; the longest document has exactly 4096 tokens.
All inputs are finite; a program needn't handle non-finite values.
Results may differ from the reference program's by a relative error of at most 0.012.
Values may be sent and summed in bfloat16 or wider, within the bound.
A program may use at most 128 MiB of HBM per device.

```python
import math
import jax
import jax.numpy as jnp
import numpy as np
from jax import lax

HD = 128
QH = 64
KVH = 4
DW = 8192
TOK_DEV = 128
DOCS = 4
TOKENS = 8192
N_PIPE = 4
N_CTX = 16
N_TP = 4


def shared_keys(key):
    base_keys = jax.random.normal(jax.random.fold_in(key, 11), (TOKENS, KVH, HD), jnp.float32) * 1.3
    base_keys = jnp.clip(base_keys, -5.5, 5.5)
    return base_keys


def draw_key_rows(key, part):
    return shared_keys(key).astype(jnp.bfloat16)


def draw_query_rows(key, part):
    drawn_query = jax.random.normal(jax.random.fold_in(key, 12), (TOKENS, QH, HD), jnp.float32) * 1.5
    drawn_query = jnp.clip(drawn_query, -9.0, 9.0)
    return drawn_query.astype(jnp.bfloat16)


def level_of(stream_key, shape, split, low, largest):
    def one(axis_at, shards_of):
        heights = jax.random.uniform(jax.random.fold_in(jax.random.fold_in(stream_key, 6), axis_at), (shards_of,), jnp.float32, low / len(split), largest / len(split))
        return jnp.repeat(jnp.exp(heights), shape[axis_at] // shards_of).reshape((-1,) + (1,) * (len(shape) - axis_at - 1))

    level = one(*split[0])
    for cut in split[1:]:
        level = level * one(*cut)
    return level


def split_up(number_of, total, limit, lean):
    portions = [(1 << 20) // math.isqrt(rank ** lean) + 1 for rank in range(2, number_of + 1)]
    rest, given = total - limit - (number_of - 1), [1] * (number_of - 1)
    while rest > 0:
        movable = [i for i in range(number_of - 1) if given[i] < limit]
        mass, budget = sum([portions[i] for i in movable]), rest
        for i in movable:
            addition = min(limit - given[i], max(1, budget * portions[i] // mass), rest)
            given[i] = given[i] + addition
            rest = rest - addition
    return np.array([limit] + given)


def ragged_sizes(own_key, number_of, total, reach, slope):
    if number_of == 2:
        one = jax.random.randint(own_key, (), max(1, total - reach), min(reach, total - 1) + 1)
        return jnp.stack([one, total - one])
    tallies = jnp.asarray(split_up(number_of, total, reach, slope), jnp.int32)
    pairs = (number_of - 1) // 2
    donor, sink = tallies[1:1 + 2 * pairs:2], tallies[2:2 + 2 * pairs:2]
    margin = jnp.minimum(donor - 1, reach - sink)
    passed = jax.random.randint(jax.random.fold_in(own_key, 1), (pairs,), 0, 1 << 20) % (margin + 1)
    tallies = tallies.at[1:1 + 2 * pairs:2].set(donor - passed).at[2:2 + 2 * pairs:2].set(sink + passed)
    return tallies[jax.random.permutation(jax.random.fold_in(own_key, 2), number_of)]


def scatter_about(rng, extent, width, most, shards=(), kind=jnp.bfloat16):
    gain = level_of(rng, extent, shards, -0.22, 0.18) if shards else 1.0
    array = jax.random.normal(rng, extent, jnp.float32) * width * gain
    return jnp.minimum(jnp.maximum(array, -most), most).astype(kind)


def setup_inputs(seed: int = 0) -> dict:
    key_list = jax.random.split(jax.random.key(seed), 6)
    return {
        "query_rows": draw_query_rows(jax.random.fold_in(key_list[5], 71), 0),
        "key_rows": draw_key_rows(jax.random.fold_in(key_list[5], 71), 0),
        "value_rows": scatter_about(key_list[2], (TOKENS, KVH, HD), 1.0, 6.0, ((0, 64), (1, 4))),
        "doc_ids": jnp.searchsorted(jnp.cumsum(ragged_sizes(key_list[3], DOCS, TOKENS, TOKENS // 2, 0)), jnp.arange(TOKENS), side="right").astype(jnp.int32),
        "out_weight": scatter_about(key_list[4], (QH * HD, DW), (QH * HD // 16) ** -0.5, 0.25, ((0, 4), (1, 16))),
    }


def reference(query_rows, key_rows, value_rows, doc_ids, out_weight):
    group_size = QH // KVH
    inv_scale = HD ** -0.5
    block_rows = math.gcd(TOKENS, 512)
    pieces = []
    for row_begin in range(0, TOKENS, block_rows):
        row_end = row_begin + block_rows
        query_pos = jnp.arange(row_begin, row_end, dtype=jnp.int32)
        key_pos = jnp.arange(row_end, dtype=jnp.int32)
        allowed = (key_pos[None, :] <= query_pos[:, None]) & (doc_ids[None, :row_end] == doc_ids[row_begin:row_end][:, None])
        query_block = query_rows[row_begin:row_end].reshape(block_rows, KVH, group_size, HD).astype(jnp.float32)
        key_block = key_rows[:row_end].astype(jnp.float32)
        value_block = value_rows[:row_end].astype(jnp.float32)

        def per_head(head_index):
            query_head = lax.dynamic_index_in_dim(query_block, head_index, 1, keepdims=False)
            key_head = lax.dynamic_index_in_dim(key_block, head_index, 1, keepdims=False)
            value_head = lax.dynamic_index_in_dim(value_block, head_index, 1, keepdims=False)
            scores = jnp.einsum("bgd,kd->gbk", query_head, key_head) * inv_scale
            masked = jnp.where(allowed[None], scores, -1e30)
            row_peak = jnp.max(masked, axis=2, keepdims=True)
            weights = jnp.where(allowed[None], jnp.exp(scores - row_peak), 0.0)
            row_total = jnp.sum(weights, axis=2)
            rounded = lax.optimization_barrier(weights.astype(jnp.bfloat16)).astype(jnp.float32)
            combined = jnp.einsum("gbk,kd->bgd", rounded, value_head)
            return combined / jnp.transpose(row_total)[:, :, None]

        per_heads = lax.map(per_head, jnp.arange(KVH, dtype=jnp.int32))
        pieces.append(jnp.transpose(per_heads, (1, 0, 2, 3)).reshape(block_rows, QH * HD).astype(jnp.bfloat16))
    attention = jnp.concatenate(pieces, axis=0)
    projected = jnp.dot(attention, out_weight, preferred_element_type=jnp.float32).astype(jnp.bfloat16)
    return projected.reshape(N_PIPE, N_CTX, N_TP, TOK_DEV // N_TP, DW)
```

```python
import functools
import math

import jax
import jax.numpy as jnp
from jax import lax
from jax.experimental import pallas as pl
from jax.experimental.pallas import tpu as pltpu
from jax.sharding import PartitionSpec as P

MESH = pl.DeviceIdType.MESH
F32 = jnp.float32
BF16 = jnp.bfloat16
NZ = 8
BLK = 128
NSLOT = 5
KROWS = NSLOT * BLK
DROW = 2 * KROWS
BROWS = DROW + NSLOT * 16
SPLIT = BROWS // 2 // 16 * 16
NEG = -1e30


def place():
    pipe = lax.axis_index("pipe")
    ctx = lax.axis_index("ctx")
    y_hi, core = pipe // 2, pipe % 2
    y_lo, z = ctx // NZ, ctx % NZ
    return y_hi, core, y_lo, z


def at(y_hi, core, y_lo, z):
    return {"pipe": y_hi * 2 + core, "ctx": y_lo * NZ + z}


def y_shift(y_hi, y_lo, step):
    y = (y_hi * 2 + y_lo + step) % 4
    return y // 2, y % 2


def octet_dev(o, z):
    return {"pipe": o // 2, "ctx": (o % 2) * NZ + z}


def attend_kernel(
    q_ref, k_ref, v_ref, d_ref, w_ref, att_ref, wo_ref, buf, m_sc, acc, qd_sc,
    a_send, a_recv, r_send, r_recv, w_send, w_recv,
):
    y_hi, core, y_lo, z = place()
    o = y_hi * 4 + core * 2 + y_lo
    up, down = at(y_hi, core, y_lo, (z + 1) % NZ), at(y_hi, core, y_lo, (z + NZ - 1) % NZ)
    yp = y_shift(y_hi, y_lo, 1)
    ym = y_shift(y_hi, y_lo, 3)
    y_up, y_down = at(yp[0], core, yp[1], z), at(ym[0], core, ym[1], z)

    barrier = pltpu.get_barrier_semaphore()
    for peer in (up, down, y_up, y_down):
        pl.semaphore_signal(barrier, inc=1, device_id=peer, device_id_type=MESH)
    for dlt in range(1, NSLOT):
        @pl.when(o - dlt >= 0)
        def _(dlt=dlt):
            pl.semaphore_signal(barrier, inc=1, device_id=octet_dev(o - dlt, z), device_id_type=MESH)

    docs = d_ref[...]
    buf[z, 0:BLK, :] = k_ref[...]
    buf[z, KROWS : KROWS + BLK, :] = v_ref[...]
    buf[z, DROW : DROW + 16, :] = jnp.broadcast_to(docs.astype(F32), (16, BLK)).astype(BF16)
    for dlt in range(1, NSLOT):
        @pl.when(o - dlt < 0)
        def _(dlt=dlt):
            zero = jnp.zeros((BLK, BLK), BF16)
            buf[z, dlt * BLK : (dlt + 1) * BLK, :] = zero
            buf[z, KROWS + dlt * BLK : KROWS + (dlt + 1) * BLK, :] = zero
            buf[z, DROW + dlt * 16 : DROW + (dlt + 1) * 16, :] = jnp.full((16, BLK), -1.0, BF16)

    pl.semaphore_wait(barrier, 4 + jnp.minimum(7 - o, 4))

    w_half = w_ref.shape[0] // 2

    def w_copy(half, dev):
        rows = pl.ds(half * w_half, w_half)
        return pltpu.make_async_remote_copy(
            w_ref.at[rows], wo_ref.at[rows], w_send.at[half], w_recv.at[half],
            device_id=dev, device_id_type=MESH,
        )

    def column_copy(dlt, part, dev):
        if part == 0:
            src, dst, n = 0, dlt * BLK, BLK
        elif part == 1:
            src, dst, n = KROWS, KROWS + dlt * BLK, BLK
        else:
            src, dst, n = DROW, DROW + dlt * 16, 16
        return pltpu.make_async_remote_copy(
            buf.at[z, pl.ds(src, n)], buf.at[z, pl.ds(dst, n)],
            a_send.at[dlt - 1, part], a_recv.at[dlt - 1, part],
            device_id=dev, device_id_type=MESH,
        )

    for dlt in range(1, NSLOT):
        @pl.when(o + dlt <= 7)
        def _(dlt=dlt):
            for part in range(3):
                column_copy(dlt, part, octet_dev(o + dlt, z)).start()
    w_copy(0, y_up).start()
    w_copy(1, y_down).start()

    r_i = lax.broadcasted_iota(jnp.int32, (BLK, BLK), 0)
    c_i = lax.broadcasted_iota(jnp.int32, (BLK, BLK), 1)
    qd_sc[...] = jnp.broadcast_to(
        jnp.sum(jnp.where(r_i == c_i, jnp.broadcast_to(docs.astype(F32), (BLK, BLK)), 0.0), axis=1, keepdims=True),
        (BLK, BLK),
    )

    def ring_copy(direction, hop, part):
        if direction == 0:
            src_z, dev = (z - (hop - 1) + NZ) % NZ, up
        else:
            src_z, dev = (z + (hop - 1)) % NZ, down
        rows = pl.ds(0, SPLIT) if part == 0 else pl.ds(SPLIT, BROWS - SPLIT)
        return pltpu.make_async_remote_copy(
            buf.at[src_z, rows], buf.at[src_z, rows],
            r_send.at[direction, hop - 1, part], r_recv.at[direction, hop - 1, part],
            device_id=dev, device_id_type=MESH,
        )

    def ring_wait(direction, hop, part):
        ring_copy(direction, hop, part).wait_recv()

    for dlt in range(1, NSLOT):
        @pl.when(o - dlt >= 0)
        def _(dlt=dlt):
            for part in range(3):
                column_copy(dlt, part, octet_dev(o, z)).wait_recv()

    for direction in range(2):
        for part in range(2):
            ring_copy(direction, 1, part).start()

    rows_total = q_ref.shape[0]
    RB = 256
    coef = (BLK ** -0.5) * math.log2(math.e)
    ones = jnp.ones

    def chunk(zz, start, nblk, own):
        n = nblk * BLK
        kd = jnp.concatenate(
            [buf[zz, pl.ds(DROW + (start + i) * 16, 16), :][0:1].astype(F32) for i in range(nblk)], axis=1
        )

        def body(rb, carry):
            rows = pl.ds(rb * RB, RB)
            q = q_ref[rows, :]
            k = buf[zz, pl.ds(start * BLK, n), :]
            v = buf[zz, pl.ds(KROWS + start * BLK, n), :]
            s = lax.dot_general(q, k, (((1,), (1,)), ((), ())), preferred_element_type=F32) * coef
            qd = qd_sc[:, 0:1]
            qd = jnp.concatenate([qd] * (RB // BLK), axis=0)
            mask = kd == qd
            if own:
                ri = lax.broadcasted_iota(jnp.int32, (RB, n), 0) % BLK
                ci = lax.broadcasted_iota(jnp.int32, (RB, n), 1)
                mask = mask & ((ci <= ri) | (ci >= BLK))
            s = jnp.where(mask, s, NEG)
            top = jnp.max(s, axis=1, keepdims=True)
            va = jnp.concatenate([v, jnp.ones((n, BLK), BF16)], axis=1)
            if own:
                m_new = top
                p = jnp.exp2(s - m_new)
                acc[rows, :] = jnp.dot(p.astype(BF16), va, preferred_element_type=F32)
            else:
                m_old = m_sc[rows, 0:1]
                m_new = jnp.maximum(m_old, top)
                alpha = jnp.exp2(m_old - m_new)
                p = jnp.exp2(s - m_new)
                acc[rows, :] = acc[rows, :] * alpha + jnp.dot(p.astype(BF16), va, preferred_element_type=F32)
            m_sc[rows, :] = jnp.broadcast_to(m_new, (RB, BLK))
            return carry

        lax.fori_loop(0, rows_total // RB, body, 0)

    chunk(z, 0, NSLOT, True)

    def steps(hop, carry):
        for direction in range(2):
            for part in range(2):
                ring_wait(direction, hop, part)
        for direction in range(2):
            ring_copy(direction, hop + 1, direction).start()

            @pl.when(hop < 3)
            def _(direction=direction):
                ring_copy(direction, hop + 1, 1 - direction).start()

        def one(i, c):
            zz = (z + jnp.where(i == 0, NZ - hop, hop)) % NZ
            chunk(zz, jnp.where(zz < z, 0, 1), NSLOT - 1, False)
            return c

        lax.fori_loop(0, 2, one, 0)
        return carry

    lax.fori_loop(1, 4, steps, 0)
    ring_wait(0, 4, 0)
    ring_wait(1, 4, 1)
    far = (z + 4) % NZ
    chunk(far, jnp.where(far < z, 0, 1), NSLOT - 1, False)

    for h in range(rows_total // BLK):
        rows = slice(h * BLK, (h + 1) * BLK)
        att_ref[:, rows] = (acc[rows, 0:BLK] / acc[rows, BLK : 2 * BLK]).astype(BF16)

    for dlt in range(1, NSLOT):
        @pl.when(o + dlt <= 7)
        def _(dlt=dlt):
            for part in range(3):
                column_copy(dlt, part, octet_dev(o, z)).wait_send()
    for direction in range(2):
        for hop in range(1, 5):
            for part in range(2):
                if hop < 4 or part == direction:
                    ring_copy(direction, hop, part).wait_send()
    for half in range(2):
        w_copy(half, y_up).wait()


def attend(q, k, v, docs, w):
    rows = q.shape[0]
    return pl.pallas_call(
        attend_kernel,
        name="gather_attend",
        out_shape=(
            jax.ShapeDtypeStruct((BLK, rows), BF16),
            jax.ShapeDtypeStruct(w.shape, BF16),
        ),
        in_specs=[pl.BlockSpec(memory_space=pltpu.VMEM)] * 4 + [pl.BlockSpec(memory_space=pl.ANY)],
        out_specs=(pl.BlockSpec(memory_space=pltpu.VMEM), pl.BlockSpec(memory_space=pl.ANY)),
        scratch_shapes=[
            pltpu.VMEM((NZ, BROWS, BLK), BF16),
            pltpu.VMEM((rows, BLK), F32),
            pltpu.VMEM((rows, 2 * BLK), F32),
            pltpu.VMEM((BLK, BLK), F32),
            pltpu.SemaphoreType.DMA((4, 3)),
            pltpu.SemaphoreType.DMA((4, 3)),
            pltpu.SemaphoreType.DMA((2, 4, 2)),
            pltpu.SemaphoreType.DMA((2, 4, 2)),
            pltpu.SemaphoreType.DMA((2,)),
            pltpu.SemaphoreType.DMA((2,)),
        ],
        compiler_params=pltpu.CompilerParams(
            collective_id=0, has_side_effects=True, vmem_limit_bytes=48 * 2**20
        ),
    )(q, k, v, docs, w)


def project_kernel(
    att_ref, w_ref, wo_ref, out_ref, ring, wv, part, got, fin,
    w_sem, own_sem, r_send, r_recv, x_send, x_recv, y_send, y_recv,
):
    y_hi, core, y_lo, z = place()
    tp = lax.axis_index("tp")
    up, down = at(y_hi, core, y_lo, (z + 1) % NZ), at(y_hi, core, y_lo, (z + NZ - 1) % NZ)
    mate = at(y_hi, core, 1 - y_lo, z)
    n_tok, depth = att_ref.shape
    feats = w_ref.shape[1]
    quarter = n_tok // 4

    barrier = pltpu.get_barrier_semaphore()
    for peer in (up, down, mate):
        pl.semaphore_signal(barrier, inc=1, device_id=peer, device_id_type=MESH)
    for i in range(1, 4):
        pl.semaphore_signal(barrier, inc=1, device_id={"tp": (tp + i) % 4}, device_id_type=MESH)
    pltpu.make_async_copy(w_ref, wv.at[0], w_sem.at[0]).start()
    pltpu.make_async_copy(wo_ref, wv.at[1], w_sem.at[1]).start()
    ring[z] = att_ref[...]
    pl.semaphore_wait(barrier, 6)

    half = n_tok // 2

    def ring_copy(direction, hop, piece):
        if direction == 0:
            src_z, dev = (z - (hop - 1) + NZ) % NZ, up
        else:
            src_z, dev = (z + (hop - 1)) % NZ, down
        rows = pl.ds(piece * half, half)
        return pltpu.make_async_remote_copy(
            ring.at[src_z, rows], ring.at[src_z, rows],
            r_send.at[direction, hop - 1, piece], r_recv.at[direction, hop - 1, piece],
            device_id=dev, device_id_type=MESH,
        )

    for direction in range(2):
        for piece in range(2):
            ring_copy(direction, 1, piece).start()

    pltpu.make_async_copy(w_ref, wv.at[0], w_sem.at[0]).wait()
    pltpu.make_async_copy(wo_ref, wv.at[1], w_sem.at[1]).wait()

    def x_copy(zz, i):
        to = (tp + i) % 4
        return pltpu.make_async_remote_copy(
            part.at[zz, to], got.at[zz, i - 1], x_send.at[zz, i - 1], x_recv.at[zz, i - 1],
            device_id={"tp": to}, device_id_type=MESH,
        )

    def y_copy(zz):
        return pltpu.make_async_remote_copy(
            fin.at[zz], out_ref.at[y_lo * NZ + zz], y_send.at[zz], y_recv.at[zz],
            device_id=mate, device_id_type=MESH,
        )

    NT = 256

    def multiply(zz):
        def cols(j, c):
            for wh in range(2):
                lanes = pl.ds(pl.multiple_of(j * NT, NT), NT)
                res = jnp.dot(ring[zz], wv[wh, :, lanes], preferred_element_type=F32).astype(BF16)
                for t in range(4):
                    part[zz, t, wh, :, lanes] = res[t * quarter : (t + 1) * quarter]
            return c

        lax.fori_loop(0, feats // NT, cols, 0)
        for i in range(1, 4):
            x_copy(zz, i).start()

    def reduce(zz):
        for i in range(1, 4):
            x_copy(zz, i).wait_recv()
        total = part[zz, tp].astype(F32)
        for i in range(3):
            total = total + got[zz, i].astype(F32)
        total = total.astype(BF16)
        out_ref[y_lo * NZ + zz] = total[0]
        fin[zz] = total[1]
        y_copy(zz).start()

    multiply(z)

    def steps(hop, carry):
        for direction in range(2):
            for piece in range(2):
                ring_copy(direction, hop, piece).wait_recv()
        for direction in range(2):
            ring_copy(direction, hop + 1, direction).start()

            @pl.when(hop < 3)
            def _(direction=direction):
                ring_copy(direction, hop + 1, 1 - direction).start()

        def one(i, c):
            zz = (z + jnp.where(i == 0, NZ - hop, hop)) % NZ
            multiply(zz)
            before = (z + jnp.where(i == 0, hop - 1, NZ - hop)) % NZ
            reduce(before)
            return c

        lax.fori_loop(0, 2, one, 0)
        return carry

    lax.fori_loop(1, 4, steps, 0)
    ring_copy(0, 4, 0).wait_recv()
    ring_copy(1, 4, 1).wait_recv()
    multiply((z + 4) % NZ)
    reduce((z + 3) % NZ)
    reduce((z + 4) % NZ)

    def drain(zz, c):
        y_copy(zz).wait()
        for i in range(1, 4):
            x_copy(zz, i).wait_send()
        return c

    lax.fori_loop(0, NZ, drain, 0)
    for direction in range(2):
        for hop in range(1, 5):
            for piece in range(2):
                if hop < 4 or piece == direction:
                    ring_copy(direction, hop, piece).wait_send()


def project(att, w, wo):
    n_tok, depth = att.shape
    feats = w.shape[1]
    quarter = n_tok // 4
    return pl.pallas_call(
        project_kernel,
        name="gather_project",
        out_shape=jax.ShapeDtypeStruct((2 * NZ, quarter, feats), BF16),
        in_specs=[
            pl.BlockSpec(memory_space=pltpu.VMEM),
            pl.BlockSpec(memory_space=pl.ANY),
            pl.BlockSpec(memory_space=pl.ANY),
        ],
        out_specs=pl.BlockSpec(memory_space=pltpu.VMEM),
        scratch_shapes=[
            pltpu.VMEM((NZ, n_tok, depth), BF16),
            pltpu.VMEM((2, depth, feats), BF16),
            pltpu.VMEM((NZ, 4, 2, quarter, feats), BF16),
            pltpu.VMEM((NZ, 3, 2, quarter, feats), BF16),
            pltpu.VMEM((NZ, quarter, feats), BF16),
            pltpu.SemaphoreType.DMA((2,)),
            pltpu.SemaphoreType.DMA,
            pltpu.SemaphoreType.DMA((2, 4, 2)),
            pltpu.SemaphoreType.DMA((2, 4, 2)),
            pltpu.SemaphoreType.DMA((NZ, 3)),
            pltpu.SemaphoreType.DMA((NZ, 3)),
            pltpu.SemaphoreType.DMA((NZ,)),
            pltpu.SemaphoreType.DMA((NZ,)),
        ],
        compiler_params=pltpu.CompilerParams(
            collective_id=1, has_side_effects=True, vmem_limit_bytes=48 * 2**20
        ),
    )(att, w, wo)


def shards(query_rows, key_rows, value_rows, doc_ids, out_weight):
    tokens, heads, width = query_rows.shape
    q = query_rows.transpose(1, 0, 2).reshape(heads * tokens, width)
    k = key_rows.reshape(tokens, width)
    v = value_rows.reshape(tokens, width)
    att, wo = attend(q, k, v, doc_ids.reshape(1, tokens), out_weight)
    out = project(att, out_weight, wo)
    return out.reshape(1, 2 * NZ, 1, tokens // 4, out_weight.shape[1])


def solution(mesh):
    return jax.shard_map(
        shards,
        mesh=mesh,
        in_specs=(
            P(("pipe", "ctx"), "tp", None),
            P(("pipe", "ctx"), "tp", None),
            P(("pipe", "ctx"), "tp", None),
            P(("pipe", "ctx")),
            P("tp", "ctx"),
        ),
        out_specs=P("pipe", None, "tp", None, "ctx"),
        check_vma=False,
    )
```

```python
import math

import jax
import jax.numpy as jnp
from jax import lax
from jax.experimental import pallas as pl
from jax.experimental.pallas import tpu as pltpu
from jax.sharding import PartitionSpec as P

MESH = pl.DeviceIdType.MESH
F32 = jnp.float32
BF16 = jnp.bfloat16
NZ = 8
BLK = 128
NSLOT = 5
VROW = BLK
DROW = 2 * BLK
BROWS = DROW + 16
NEG = -1e30


def fused_kernel(
    q_ref, k_ref, v_ref, d_ref, w_ref, out_ref,
    kv, qd, m_sc, acc, den, ring, wv, part, got, fin,
    wl_sem, c_send, c_recv, k_send, k_recv, y_send, y_recv, n_send, n_recv,
    w_send, w_recv, s_send, s_recv, r_send, r_recv, x_send, x_recv, f_send, f_recv,
):
    pipe, ctx, tp = lax.axis_index("pipe"), lax.axis_index("ctx"), lax.axis_index("tp")
    y_hi, core = pipe // 2, pipe % 2
    y_lo, z = ctx // NZ, ctx % NZ
    o = pipe * 2 + y_lo
    y = y_hi * 2 + y_lo
    n_row = q_ref.shape[0]
    heads = n_row // BLK
    depth, feats = w_ref.shape

    def z_dev(direction):
        return {"ctx": y_lo * NZ + (z + jnp.where(direction == 0, 1, NZ - 1)) % NZ}

    def o_dev(octet):
        return {"pipe": octet // 2, "ctx": (octet % 2) * NZ + z}

    def y_dev(step):
        to = (y + step) % 4
        return {"pipe": (to // 2) * 2 + core, "ctx": (to % 2) * NZ + z}

    sibling = {"pipe": y_hi * 2 + (1 - core)}
    mate = {"ctx": (1 - y_lo) * NZ + z}

    def signal(barrier, dev):
        pl.semaphore_signal(barrier, inc=1, device_id=dev, device_id_type=MESH)

    barrier = pltpu.get_barrier_semaphore()
    for dev in (z_dev(0), z_dev(1), y_dev(1), y_dev(3), sibling, mate):
        signal(barrier, dev)
    for i in range(1, 4):
        signal(barrier, {"tp": (tp + i) % 4})
    for dlt in range(1, NSLOT):
        @pl.when(o - dlt >= 0)
        def _(dlt=dlt):
            signal(barrier, o_dev(o - dlt))

    w_local = pltpu.make_async_copy(w_ref, wv.at[0], wl_sem)
    w_local.start()

    docs = d_ref[...].astype(F32)
    kv[z, 0, 0:BLK, :] = k_ref[...].T
    kv[z, 0, VROW : VROW + BLK, :] = v_ref[...]
    kv[z, 0, DROW:BROWS, :] = jnp.broadcast_to(docs, (16, BLK)).astype(BF16)

    pl.semaphore_wait(barrier, 9 + jnp.minimum(7 - o, 4))

    def remote(src, dst, send, recv, dev):
        return pltpu.make_async_remote_copy(src, dst, send, recv, device_id=dev, device_id_type=MESH)

    def z_copy(slot, direction, hop, far):
        src_z = (z + jnp.where(direction == 0, NZ + 1 - hop, hop - 1)) % NZ
        if far is None:
            rows = pl.ds(0, BROWS)
        else:
            rows = pl.ds(0, VROW) if far == 0 else pl.ds(VROW, BROWS - VROW)
        ref = kv.at[src_z, slot, rows]
        return remote(
            ref, ref, k_send.at[slot, direction, hop - 1], k_recv.at[slot, direction, hop - 1],
            z_dev(direction),
        )

    def col_copy(dlt):
        return remote(
            kv.at[z, 0], kv.at[z, dlt], c_send.at[dlt], c_recv.at[dlt],
            o_dev(jnp.minimum(o + dlt, 7)),
        )

    def y_copy(zz):
        return remote(
            kv.at[zz, 0], kv.at[zz, 1], y_send.at[zz], y_recv.at[zz], o_dev(jnp.minimum(o + 1, 7))
        )

    def n_copy(zz):
        return remote(kv.at[zz, 0], kv.at[zz, 2], n_send.at[zz], n_recv.at[zz], sibling)

    ring2 = (y_hi == 1) & (core == 0)
    feed2 = (y_hi == 0) & (core == 1)
    ring_slots = ((0, o >= 0), (2, ring2), (3, o >= 3), (4, o >= 4))
    cols = ((2, feed2, ring2), (3, o <= 4, o >= 3), (4, o <= 3, o >= 4))

    def pass_on(zz):
        @pl.when(o <= 6)
        def _():
            y_copy(zz).start()

        @pl.when(core == 0)
        def _():
            n_copy(zz).start()

    for direction in range(2):
        z_copy(0, direction, 1, None).start()
    for dlt, sends, _ in cols:
        @pl.when(sends)
        def _(dlt=dlt):
            col_copy(dlt).start()
    pass_on(z)

    for dlt in range(1, NSLOT):
        @pl.when(o < dlt)
        def _(dlt=dlt):
            for zz in range(NZ):
                kv[zz, dlt, 0:DROW, :] = jnp.zeros((DROW, BLK), BF16)
                kv[zz, dlt, DROW:BROWS, :] = jnp.full((16, BLK), -1.0, BF16)

    for dlt, _, takes in cols:
        @pl.when(takes)
        def _(dlt=dlt):
            col_copy(dlt).wait_recv()
            for direction in range(2):
                z_copy(dlt, direction, 1, None).start()

    r_i = lax.broadcasted_iota(jnp.int32, (n_row, BLK), 0) // heads
    c_i = lax.broadcasted_iota(jnp.int32, (n_row, BLK), 1)
    qd[...] = jnp.broadcast_to(
        jnp.sum(jnp.where(r_i == c_i, docs, 0.0), axis=1, keepdims=True), (n_row, BLK)
    )

    coef = (BLK ** -0.5) * math.log2(math.e)

    def attend(zz, start, nblk, rb, own):
        def body(i, carry):
            rows = pl.ds(pl.multiple_of(i * rb, rb), rb)
            kt = jnp.concatenate([kv[zz, start + b, 0:BLK, :] for b in range(nblk)], axis=1)
            va = jnp.concatenate([kv[zz, start + b, VROW : VROW + BLK, :] for b in range(nblk)], axis=0)
            va = jnp.concatenate([va, jnp.ones((nblk * BLK, BLK), BF16)], axis=1)
            kd = jnp.concatenate(
                [kv[zz, start + b, DROW:BROWS, :][0:1].astype(F32) for b in range(nblk)], axis=1
            )
            s = jnp.dot(q_ref[rows, :], kt, preferred_element_type=F32) * coef
            mask = kd == jnp.concatenate([qd[rows, :]] * nblk, axis=1)
            if own:
                ri = (lax.broadcasted_iota(jnp.int32, (rb, nblk * BLK), 0) + i * rb) // heads
                ci = lax.broadcasted_iota(jnp.int32, (rb, nblk * BLK), 1)
                mask = mask & ((ci <= ri) | (ci >= BLK))
            s = jnp.where(mask, s, NEG)
            top = jnp.max(s, axis=1, keepdims=True)
            if own:
                m_new = jnp.broadcast_to(top, (rb, BLK))
            else:
                m_old = m_sc[rows, :]
                m_new = jnp.maximum(m_old, top)
            p = jnp.exp2(s - jnp.concatenate([m_new] * nblk, axis=1)).astype(BF16)
            res = jnp.dot(p, va, preferred_element_type=F32)
            if own:
                acc[rows, :] = res[:, :BLK]
                den[rows, :] = res[:, BLK:]
            else:
                alpha = jnp.exp2(m_old - m_new)
                acc[rows, :] = acc[rows, :] * alpha + res[:, :BLK]
                den[rows, :] = den[rows, :] * alpha + res[:, BLK:]
            m_sc[rows, :] = m_new
            return carry

        if rb == n_row:
            body(0, 0)
        else:
            lax.fori_loop(0, n_row // rb, body, 0)

    def side_wait(zz):
        @pl.when(o >= 1)
        def _():
            y_copy(zz).wait_recv()

        @pl.when(core == 1)
        def _():
            n_copy(zz).wait_recv()

    side_wait(z)
    attend(z, 0, NSLOT, 1024, True)

    quarter_w = depth // 4

    def w_copy(i):
        rows = pl.ds((2 * i + core) * quarter_w, quarter_w)
        return remote(w_ref.at[rows], wv.at[1, rows], w_send.at[i], w_recv.at[i], y_dev(1 + 2 * i))

    def s_copy(i):
        rows = pl.ds((2 * i + core) * quarter_w, quarter_w)
        return remote(wv.at[1, rows], wv.at[1, rows], s_send.at[i], s_recv.at[i], sibling)

    def arrivals(i, carry):
        @pl.when(i < 6)
        def _():
            hop, direction = i // 2 + 1, i % 2
            zz = (z + jnp.where(direction == 0, NZ - hop, hop)) % NZ
            for slot, used in ring_slots:
                @pl.when(used)
                def _(slot=slot):
                    z_copy(slot, direction, hop, None).wait_recv()

                    @pl.when(hop < 3)
                    def _():
                        z_copy(slot, direction, hop + 1, None).start()

                    for d in range(2):
                        @pl.when((hop == 3) & (direction == d))
                        def _(d=d):
                            z_copy(slot, d, 4, d).start()

                if slot == 0:
                    pass_on(zz)

        @pl.when(i == 6)
        def _():
            for slot, used in ring_slots:
                @pl.when(used)
                def _(slot=slot):
                    for d in range(2):
                        z_copy(slot, d, 4, d).wait_recv()

                if slot == 0:
                    pass_on((z + 4) % NZ)

        @pl.when(i == 2)
        def _():
            for j in range(2):
                w_copy(j).start()

        @pl.when(i == 6)
        def _():
            for j in range(2):
                w_copy(j).wait_recv()
                s_copy(j).start()

        far = i // 2 + 1
        zz = (z + jnp.where(i % 2 == 0, NZ - far, far)) % NZ
        side_wait(zz)
        attend(zz, jnp.where(zz < z, 0, 1), NSLOT - 1, n_row, False)
        return carry

    lax.fori_loop(0, 7, arrivals, 0)

    span = BLK // 4 // 2
    for h in range(heads):
        rows = pl.ds(h, BLK, stride=heads)
        val = (acc[rows, :] / den[rows, :]).astype(BF16)
        for j in range(2):
            for t in range(4):
                ring[z, j, t * span : (t + 1) * span, h * BLK : (h + 1) * BLK] = val[
                    (2 * t + j) * span : (2 * t + j + 1) * span
                ]

    def r_copy(direction, hop, j):
        src_z = (z + jnp.where(direction == 0, NZ + 1 - hop, hop - 1)) % NZ
        ref = ring.at[src_z, j]
        return remote(
            ref, ref, r_send.at[direction, hop - 1, j], r_recv.at[direction, hop - 1, j],
            z_dev(direction),
        )

    for j in range(2):
        for direction in range(2):
            r_copy(direction, 1, j).start()

    def x_copy(s, i):
        to = (tp + i) % 4
        return remote(
            part.at[s, to], got.at[s, i - 1], x_send.at[s, i - 1], x_recv.at[s, i - 1], {"tp": to}
        )

    def where_of(s):
        hop, j = (s + 1) // 2, (s + 1) % 2
        end = (s == 0) | (s == 7)
        za = (z + jnp.where(s == 0, 0, jnp.where(s == 7, 4, NZ - hop))) % NZ
        zb = (z + jnp.where(s == 0, 0, jnp.where(s == 7, 4, hop))) % NZ
        return (za, jnp.where(end, 0, j)), (zb, jnp.where(end, 1, j))

    def f_copy(s, side, spot):
        zz, j = spot
        return remote(
            fin.at[s, pl.ds(side * span, span)],
            out_ref.at[y_lo * NZ + zz, pl.ds(pl.multiple_of(j * span, span), span)],
            f_send.at[s, side], f_recv.at[s, side], mate,
        )

    NT = 256

    def multiply(s):
        (za, ja), (zb, jb) = where_of(s)

        def cols(n, c):
            lanes = pl.ds(pl.multiple_of(n * NT, NT), NT)
            x = jnp.concatenate([ring[za, ja], ring[zb, jb]], axis=0)
            for wh in range(2):
                res = jnp.dot(x, wv[wh, :, lanes], preferred_element_type=F32).astype(BF16)
                for side in range(2):
                    for t in range(4):
                        part[s, t, wh, side * span : (side + 1) * span, lanes] = res[
                            (side * 4 + t) * span : (side * 4 + t + 1) * span
                        ]
            return c

        lax.fori_loop(0, feats // NT, cols, 0)
        for i in range(1, 4):
            x_copy(s, i).start()

    def reduce(s):
        for i in range(1, 4):
            x_copy(s, i).wait_recv()
        total = part[s, tp].astype(F32)
        for i in range(3):
            total = total + got[s, i].astype(F32)
        total = total.astype(BF16)
        fin[s] = total[1]
        for side, spot in enumerate(where_of(s)):
            f_copy(s, side, spot).start()
            out_ref[y_lo * NZ + spot[0], pl.ds(pl.multiple_of(spot[1] * span, span), span), :] = total[
                0, side * span : (side + 1) * span
            ]

    w_local.wait()
    for i in range(2):
        s_copy(i).wait_recv()
    multiply(0)

    def steps(s, carry):
        hop, j = (s + 1) // 2, (s + 1) % 2
        for direction in range(2):
            r_copy(direction, hop, j).wait_recv()

            @pl.when((hop < 3) | (j == direction))
            def _(direction=direction):
                r_copy(direction, hop + 1, j).start()

        multiply(s)

        @pl.when(s >= 2)
        def _():
            reduce(s - 2)

        return carry

    lax.fori_loop(1, 7, steps, 0)
    for d in range(2):
        r_copy(d, 4, d).wait_recv()
    multiply(7)
    for s in range(5, 8):
        reduce(s)

    def drain(s, c):
        for i in range(1, 4):
            x_copy(s, i).wait_send()
        for side, spot in enumerate(where_of(s)):
            f_copy(s, side, spot).wait()

        @pl.when(o <= 6)
        def _():
            y_copy(s).wait_send()

        @pl.when(core == 0)
        def _():
            n_copy(s).wait_send()

        return c

    lax.fori_loop(0, NZ, drain, 0)
    for direction in range(2):
        for hop in range(1, 5):
            for j in range(2):
                if hop < 4 or j == direction:
                    r_copy(direction, hop, j).wait_send()
            for slot, used in ring_slots:
                @pl.when(used)
                def _(slot=slot, direction=direction, hop=hop):
                    z_copy(slot, direction, hop, None if hop < 4 else direction).wait_send()
    for dlt, sends, _ in cols:
        @pl.when(sends)
        def _(dlt=dlt):
            col_copy(dlt).wait_send()
    for i in range(2):
        w_copy(i).wait_send()
        s_copy(i).wait_send()


def fused(q, k, v, docs, w):
    n_row = q.shape[0]
    depth, feats = w.shape
    quarter = BLK // 4
    dma = pltpu.SemaphoreType.DMA
    vmem = pl.BlockSpec(memory_space=pltpu.VMEM)
    return pl.pallas_call(
        fused_kernel,
        name="attend_project",
        out_shape=jax.ShapeDtypeStruct((2 * NZ, quarter, feats), BF16),
        in_specs=[vmem] * 4 + [pl.BlockSpec(memory_space=pl.ANY)],
        out_specs=vmem,
        scratch_shapes=[
            pltpu.VMEM((NZ, NSLOT, BROWS, BLK), BF16),
            pltpu.VMEM((n_row, BLK), F32),
            pltpu.VMEM((n_row, BLK), F32),
            pltpu.VMEM((n_row, BLK), F32),
            pltpu.VMEM((n_row, BLK), F32),
            pltpu.VMEM((NZ, 2, BLK // 2, depth), BF16),
            pltpu.VMEM((2, depth, feats), BF16),
            pltpu.VMEM((NZ, 4, 2, quarter, feats), BF16),
            pltpu.VMEM((NZ, 3, 2, quarter, feats), BF16),
            pltpu.VMEM((NZ, quarter, feats), BF16),
            dma,
            dma((NSLOT,)),
            dma((NSLOT,)),
            dma((NSLOT, 2, 4)),
            dma((NSLOT, 2, 4)),
            dma((NZ,)),
            dma((NZ,)),
            dma((NZ,)),
            dma((NZ,)),
            dma((2,)),
            dma((2,)),
            dma((2,)),
            dma((2,)),
            dma((2, 4, 2)),
            dma((2, 4, 2)),
            dma((NZ, 3)),
            dma((NZ, 3)),
            dma((NZ, 2)),
            dma((NZ, 2)),
        ],
        compiler_params=pltpu.CompilerParams(
            collective_id=0, has_side_effects=True, vmem_limit_bytes=60 * 2**20
        ),
    )(q, k, v, docs, w)


def shards(query_rows, key_rows, value_rows, doc_ids, out_weight):
    tokens, heads, width = query_rows.shape
    q = query_rows.reshape(tokens * heads, width)
    k = key_rows.reshape(tokens, width)
    v = value_rows.reshape(tokens, width)
    out = fused(q, k, v, doc_ids.reshape(1, tokens), out_weight)
    return out.reshape(1, 2 * NZ, 1, tokens // 4, out_weight.shape[1])


def solution(mesh):
    return jax.shard_map(
        shards,
        mesh=mesh,
        in_specs=(
            P(("pipe", "ctx"), "tp", None),
            P(("pipe", "ctx"), "tp", None),
            P(("pipe", "ctx"), "tp", None),
            P(("pipe", "ctx")),
            P("tp", "ctx"),
        ),
        out_specs=P("pipe", None, "tp", None, "ctx"),
        check_vma=False,
    )
```

```python
import math

import jax
import jax.numpy as jnp
from jax import lax
from jax.experimental import pallas as pl
from jax.experimental.pallas import tpu as pltpu
from jax.sharding import PartitionSpec as P

MESH = pl.DeviceIdType.MESH
F32 = jnp.float32
BF16 = jnp.bfloat16
NZ = 8
BLK = 128
NSLOT = 5
VROW = BLK
DROW = 2 * BLK
BROWS = DROW + 16
NEG = -1e30


def fused_kernel(
    q_hbm, k_ref, v_ref, d_ref, w_ref, out_ref,
    q_ref, kv, qd, m_sc, acc, den, ring, wv, part, got, fin,
    q_sem, wl_sem, c_send, c_recv, k_send, k_recv, y_send, y_recv, n_send, n_recv,
    w_send, w_recv, s_send, s_recv, r_send, r_recv, x_send, x_recv, f_send, f_recv,
):
    pipe, ctx, tp = lax.axis_index("pipe"), lax.axis_index("ctx"), lax.axis_index("tp")
    y_hi, core = pipe // 2, pipe % 2
    y_lo, z = ctx // NZ, ctx % NZ
    o = pipe * 2 + y_lo
    y = y_hi * 2 + y_lo
    n_row = q_hbm.shape[0]
    heads = n_row // BLK
    depth, feats = w_ref.shape

    def z_dev(direction):
        return {"ctx": y_lo * NZ + (z + jnp.where(direction == 0, 1, NZ - 1)) % NZ}

    def o_dev(octet):
        return {"pipe": octet // 2, "ctx": (octet % 2) * NZ + z}

    def y_dev(step):
        to = (y + step) % 4
        return {"pipe": (to // 2) * 2 + core, "ctx": (to % 2) * NZ + z}

    sibling = {"pipe": y_hi * 2 + (1 - core)}
    mate = {"ctx": (1 - y_lo) * NZ + z}

    def signal(barrier, dev):
        pl.semaphore_signal(barrier, inc=1, device_id=dev, device_id_type=MESH)

    barrier = pltpu.get_barrier_semaphore()
    for dev in (z_dev(0), z_dev(1), y_dev(1), y_dev(3), sibling, mate):
        signal(barrier, dev)
    for i in range(1, 4):
        signal(barrier, {"tp": (tp + i) % 4})
    for dlt in range(1, NSLOT):
        @pl.when(o - dlt >= 0)
        def _(dlt=dlt):
            signal(barrier, o_dev(o - dlt))

    q_local = pltpu.make_async_copy(q_hbm, q_ref, q_sem)
    q_local.start()
    w_local = pltpu.make_async_copy(w_ref, wv.at[0], wl_sem)
    w_local.start()

    docs = d_ref[...].astype(F32)
    kv[z, 0, 0:BLK, :] = k_ref[...].T
    kv[z, 0, VROW : VROW + BLK, :] = v_ref[...]
    kv[z, 0, DROW:BROWS, :] = jnp.broadcast_to(docs, (16, BLK)).astype(BF16)

    pl.semaphore_wait(barrier, 9 + jnp.minimum(7 - o, 4))

    def remote(src, dst, send, recv, dev):
        return pltpu.make_async_remote_copy(src, dst, send, recv, device_id=dev, device_id_type=MESH)

    def z_copy(slot, direction, hop, far):
        src_z = (z + jnp.where(direction == 0, NZ + 1 - hop, hop - 1)) % NZ
        if far is None:
            rows = pl.ds(0, BROWS)
        else:
            rows = pl.ds(0, VROW) if far == 0 else pl.ds(VROW, BROWS - VROW)
        ref = kv.at[src_z, slot, rows]
        return remote(
            ref, ref, k_send.at[slot, direction, hop - 1], k_recv.at[slot, direction, hop - 1],
            z_dev(direction),
        )

    def col_copy(dlt):
        return remote(
            kv.at[z, 0], kv.at[z, dlt], c_send.at[dlt], c_recv.at[dlt],
            o_dev(jnp.minimum(o + dlt, 7)),
        )

    def y_copy(zz):
        return remote(
            kv.at[zz, 0], kv.at[zz, 1], y_send.at[zz], y_recv.at[zz], o_dev(jnp.minimum(o + 1, 7))
        )

    def n_copy(zz):
        return remote(kv.at[zz, 0], kv.at[zz, 2], n_send.at[zz], n_recv.at[zz], sibling)

    ring2 = (y_hi == 1) & (core == 0)
    feed2 = (y_hi == 0) & (core == 1)
    ring_slots = ((2, ring2), (3, o >= 3), (4, o >= 4))
    cols = ((2, feed2, ring2), (3, o <= 4, o >= 3), (4, o <= 3, o >= 4))

    def pass_on(zz):
        @pl.when(o <= 6)
        def _():
            y_copy(zz).start()

        @pl.when(core == 0)
        def _():
            n_copy(zz).start()

    for direction in range(2):
        z_copy(0, direction, 1, None).start()
    for dlt, sends, _ in cols:
        @pl.when(sends)
        def _(dlt=dlt):
            col_copy(dlt).start()
    pass_on(z)

    for dlt in range(1, NSLOT):
        @pl.when(o < dlt)
        def _(dlt=dlt):
            for zz in range(NZ):
                kv[zz, dlt, 0:DROW, :] = jnp.zeros((DROW, BLK), BF16)
                kv[zz, dlt, DROW:BROWS, :] = jnp.full((16, BLK), -1.0, BF16)

    r_i = lax.broadcasted_iota(jnp.int32, (n_row, BLK), 0) // heads
    c_i = lax.broadcasted_iota(jnp.int32, (n_row, BLK), 1)
    qd[...] = jnp.broadcast_to(
        jnp.sum(jnp.where(r_i == c_i, docs, 0.0), axis=1, keepdims=True), (n_row, BLK)
    )

    coef = (BLK ** -0.5) * math.log2(math.e)

    def attend(zz, start, nblk, rb, own):
        def body(i, carry):
            rows = pl.ds(pl.multiple_of(i * rb, rb), rb)
            kt = jnp.concatenate([kv[zz, start + b, 0:BLK, :] for b in range(nblk)], axis=1)
            va = jnp.concatenate([kv[zz, start + b, VROW : VROW + BLK, :] for b in range(nblk)], axis=0)
            va = jnp.concatenate([va, jnp.ones((nblk * BLK, BLK), BF16)], axis=1)
            kd = jnp.concatenate(
                [kv[zz, start + b, DROW:BROWS, :][0:1].astype(F32) for b in range(nblk)], axis=1
            )
            s = jnp.dot(q_ref[rows, :], kt, preferred_element_type=F32) * coef
            mask = kd == jnp.concatenate([qd[rows, :]] * nblk, axis=1)
            if own:
                ri = (lax.broadcasted_iota(jnp.int32, (rb, nblk * BLK), 0) + i * rb) // heads
                ci = lax.broadcasted_iota(jnp.int32, (rb, nblk * BLK), 1)
                mask = mask & ((ci <= ri) | (ci >= BLK))
            s = jnp.where(mask, s, NEG)
            top = jnp.max(s, axis=1, keepdims=True)
            if own:
                m_new = jnp.broadcast_to(top, (rb, BLK))
            else:
                m_old = m_sc[rows, :]
                m_new = jnp.maximum(m_old, top)
            p = jnp.exp2(s - jnp.concatenate([m_new] * nblk, axis=1)).astype(BF16)
            res = jnp.dot(p, va, preferred_element_type=F32)
            if own:
                acc[rows, :] = res[:, :BLK]
                den[rows, :] = res[:, BLK:]
            else:
                alpha = jnp.exp2(m_old - m_new)
                acc[rows, :] = acc[rows, :] * alpha + res[:, :BLK]
                den[rows, :] = den[rows, :] * alpha + res[:, BLK:]
            m_sc[rows, :] = m_new
            return carry

        if rb == n_row:
            body(0, 0)
        else:
            lax.fori_loop(0, n_row // rb, body, 0)

    def side_wait(zz):
        @pl.when(o >= 1)
        def _():
            y_copy(zz).wait_recv()

        @pl.when(core == 1)
        def _():
            n_copy(zz).wait_recv()

    quarter_w = depth // 4

    def w_copy(i):
        rows = pl.ds((2 * i + core) * quarter_w, quarter_w)
        return remote(w_ref.at[rows], wv.at[1, rows], w_send.at[i], w_recv.at[i], y_dev(1 + 2 * i))

    def s_copy(i):
        rows = pl.ds((2 * i + core) * quarter_w, quarter_w)
        return remote(wv.at[1, rows], wv.at[1, rows], s_send.at[i], s_recv.at[i], sibling)

    def forward(slot, hop):
        for d in range(2):
            z_copy(slot, d, hop, None).wait_recv()

            @pl.when(hop < 3)
            def _(d=d):
                z_copy(slot, d, hop + 1, None).start()

            @pl.when(hop == 3)
            def _(d=d):
                z_copy(slot, d, 4, d).start()

    def last(slot):
        for d in range(2):
            z_copy(slot, d, 4, d).wait_recv()

    def own_octet(hop):
        @pl.when(hop < 4)
        def _():
            forward(0, hop)
            pass_on((z + hop) % NZ)
            pass_on((z + NZ - hop) % NZ)

        @pl.when(hop == 4)
        def _():
            last(0)
            pass_on((z + 4) % NZ)

    own_octet(jnp.int32(1))
    for dlt, _, takes in cols:
        @pl.when(takes)
        def _(dlt=dlt):
            col_copy(dlt).wait_recv()
            for direction in range(2):
                z_copy(dlt, direction, 1, None).start()

    q_local.wait()
    side_wait(z)
    attend(z, 0, NSLOT, 1024, True)

    def arrivals(hop, carry):
        @pl.when(hop < 4)
        def _():
            own_octet(hop + 1)

        for slot, used in ring_slots:
            @pl.when(used)
            def _(slot=slot):
                @pl.when(hop < 4)
                def _():
                    forward(slot, hop)

                @pl.when(hop == 4)
                def _():
                    last(slot)

        @pl.when(hop == 4)
        def _():
            for j in range(2):
                w_copy(j).start()

        def one(i, c):
            zz = (z + jnp.where(i == 0, NZ - hop, hop)) % NZ
            side_wait(zz)
            attend(zz, jnp.where(zz < z, 0, 1), NSLOT - 1, n_row, False)
            return c

        lax.fori_loop(0, jnp.where(hop == 4, 1, 2), one, 0)
        return carry

    lax.fori_loop(1, 5, arrivals, 0)

    span = BLK // 4 // 2
    for h in range(heads):
        rows = pl.ds(h, BLK, stride=heads)
        val = (acc[rows, :] / den[rows, :]).astype(BF16)
        for j in range(2):
            for t in range(4):
                ring[z, j, t * span : (t + 1) * span, h * BLK : (h + 1) * BLK] = val[
                    (2 * t + j) * span : (2 * t + j + 1) * span
                ]

    def r_copy(direction, hop, j):
        src_z = (z + jnp.where(direction == 0, NZ + 1 - hop, hop - 1)) % NZ
        ref = ring.at[src_z, j]
        return remote(
            ref, ref, r_send.at[direction, hop - 1, j], r_recv.at[direction, hop - 1, j],
            z_dev(direction),
        )

    for j in range(2):
        for direction in range(2):
            r_copy(direction, 1, j).start()

    def x_copy(s, wh, i):
        to = (tp + i) % 4
        return remote(
            part.at[s, wh, to], got.at[s, wh, i - 1],
            x_send.at[s, wh, i - 1], x_recv.at[s, wh, i - 1], {"tp": to},
        )

    def where_of(s):
        hop, j = (s + 1) // 2, (s + 1) % 2
        end = (s == 0) | (s == 7)
        za = (z + jnp.where(s == 0, 0, jnp.where(s == 7, 4, NZ - hop))) % NZ
        zb = (z + jnp.where(s == 0, 0, jnp.where(s == 7, 4, hop))) % NZ
        return (za, jnp.where(end, 0, j)), (zb, jnp.where(end, 1, j))

    def f_copy(s, side, spot):
        zz, j = spot
        return remote(
            fin.at[s, pl.ds(side * span, span)],
            out_ref.at[y_lo * NZ + zz, pl.ds(pl.multiple_of(j * span, span), span)],
            f_send.at[s, side], f_recv.at[s, side], mate,
        )

    NT = 256

    def multiply(s, wh):
        (za, ja), (zb, jb) = where_of(s)

        def cols(n, c):
            lanes = pl.ds(pl.multiple_of(n * NT, NT), NT)
            x = jnp.concatenate([ring[za, ja], ring[zb, jb]], axis=0)
            res = jnp.dot(x, wv[wh, :, lanes], preferred_element_type=F32).astype(BF16)
            for side in range(2):
                for t in range(4):
                    part[s, wh, t, side * span : (side + 1) * span, lanes] = res[
                        (side * 4 + t) * span : (side * 4 + t + 1) * span
                    ]
            return c

        lax.fori_loop(0, feats // NT, cols, 0)
        for i in range(1, 4):
            x_copy(s, wh, i).start()

    def reduce(s):
        sums = []
        for wh in (1, 0):
            for i in range(1, 4):
                x_copy(s, wh, i).wait_recv()
            total = part[s, wh, tp].astype(F32)
            for i in range(3):
                total = total + got[s, wh, i].astype(F32)
            total = total.astype(BF16)
            for side, spot in enumerate(where_of(s)):
                if wh == 1:
                    if side == 0:
                        fin[s] = total
                    f_copy(s, side, spot).start()
                else:
                    out_ref[y_lo * NZ + spot[0], pl.ds(pl.multiple_of(spot[1] * span, span), span), :] = total[
                        side * span : (side + 1) * span
                    ]

    w_local.wait()
    multiply(0, 0)

    def run(fn, lo, hi):
        def body(i, c):
            fn(i)
            return c

        lax.fori_loop(lo, hi, body, 0)

    LATE = 3

    def steps(s, carry):
        hop, j = (s + 1) // 2, (s + 1) % 2
        for direction in range(2):
            r_copy(direction, hop, j).wait_recv()

            @pl.when((hop < 3) | (j == direction))
            def _(direction=direction):
                r_copy(direction, hop + 1, j).start()

        @pl.when(s == LATE - 1)
        def _():
            for i in range(2):
                w_copy(i).wait_recv()
                s_copy(i).start()

        @pl.when(s == LATE)
        def _():
            for i in range(2):
                s_copy(i).wait_recv()

        first = jnp.where(s < LATE, s, jnp.where(s == LATE, 0, s))
        run(lambda i: multiply(jnp.where(i == 0, s, first + i - 1), jnp.where(i == 0, 0, 1)), 0,
            jnp.where(s < LATE, 1, s - first + 2))
        run(reduce, jnp.where(s == LATE + 1, 0, s - 2), jnp.where(s <= LATE, s - 2, s - 1))
        return carry

    lax.fori_loop(1, 7, steps, 0)
    for d in range(2):
        r_copy(d, 4, d).wait_recv()
    run(lambda i: multiply(7, i), 0, 2)
    run(reduce, 5, 8)

    def drain(s, c):
        for wh in range(2):
            for i in range(1, 4):
                x_copy(s, wh, i).wait_send()
        for side, spot in enumerate(where_of(s)):
            f_copy(s, side, spot).wait()

        @pl.when(o <= 6)
        def _():
            y_copy(s).wait_send()

        @pl.when(core == 0)
        def _():
            n_copy(s).wait_send()

        return c

    lax.fori_loop(0, NZ, drain, 0)
    for direction in range(2):
        for hop in range(1, 5):
            for j in range(2):
                if hop < 4 or j == direction:
                    r_copy(direction, hop, j).wait_send()
            for slot, used in ((0, o >= 0),) + ring_slots:
                @pl.when(used)
                def _(slot=slot, direction=direction, hop=hop):
                    z_copy(slot, direction, hop, None if hop < 4 else direction).wait_send()
    for dlt, sends, _ in cols:
        @pl.when(sends)
        def _(dlt=dlt):
            col_copy(dlt).wait_send()
    for i in range(2):
        w_copy(i).wait_send()
        s_copy(i).wait_send()


def fused(q, k, v, docs, w):
    n_row = q.shape[0]
    depth, feats = w.shape
    quarter = BLK // 4
    dma = pltpu.SemaphoreType.DMA
    vmem = pl.BlockSpec(memory_space=pltpu.VMEM)
    return pl.pallas_call(
        fused_kernel,
        name="attend_project",
        out_shape=jax.ShapeDtypeStruct((2 * NZ, quarter, feats), BF16),
        in_specs=[pl.BlockSpec(memory_space=pl.ANY)] + [vmem] * 3 + [pl.BlockSpec(memory_space=pl.ANY)],
        out_specs=vmem,
        scratch_shapes=[
            pltpu.VMEM((n_row, BLK), BF16),
            pltpu.VMEM((NZ, NSLOT, BROWS, BLK), BF16),
            pltpu.VMEM((n_row, BLK), F32),
            pltpu.VMEM((n_row, BLK), F32),
            pltpu.VMEM((n_row, BLK), F32),
            pltpu.VMEM((n_row, BLK), F32),
            pltpu.VMEM((NZ, 2, BLK // 2, depth), BF16),
            pltpu.VMEM((2, depth, feats), BF16),
            pltpu.VMEM((NZ, 2, 4, quarter, feats), BF16),
            pltpu.VMEM((NZ, 2, 3, quarter, feats), BF16),
            pltpu.VMEM((NZ, quarter, feats), BF16),
            dma,
            dma,
            dma((NSLOT,)),
            dma((NSLOT,)),
            dma((NSLOT, 2, 4)),
            dma((NSLOT, 2, 4)),
            dma((NZ,)),
            dma((NZ,)),
            dma((NZ,)),
            dma((NZ,)),
            dma((2,)),
            dma((2,)),
            dma((2,)),
            dma((2,)),
            dma((2, 4, 2)),
            dma((2, 4, 2)),
            dma((NZ, 2, 3)),
            dma((NZ, 2, 3)),
            dma((NZ, 2)),
            dma((NZ, 2)),
        ],
        compiler_params=pltpu.CompilerParams(
            collective_id=0, has_side_effects=True, vmem_limit_bytes=60 * 2**20
        ),
    )(q, k, v, docs, w)


def shards(query_rows, key_rows, value_rows, doc_ids, out_weight):
    tokens, heads, width = query_rows.shape
    q = query_rows.reshape(tokens * heads, width)
    k = key_rows.reshape(tokens, width)
    v = value_rows.reshape(tokens, width)
    out = fused(q, k, v, doc_ids.reshape(1, tokens), out_weight)
    return out.reshape(1, 2 * NZ, 1, tokens // 4, out_weight.shape[1])


def solution(mesh):
    return jax.shard_map(
        shards,
        mesh=mesh,
        in_specs=(
            P(("pipe", "ctx"), "tp", None),
            P(("pipe", "ctx"), "tp", None),
            P(("pipe", "ctx"), "tp", None),
            P(("pipe", "ctx")),
            P("tp", "ctx"),
        ),
        out_specs=P("pipe", None, "tp", None, "ctx"),
        check_vma=False,
    )
```

```python
import math

import jax
import jax.numpy as jnp
from jax import lax
from jax.experimental import pallas as pl
from jax.experimental.pallas import tpu as pltpu
from jax.sharding import PartitionSpec as P

MESH = pl.DeviceIdType.MESH
F32 = jnp.float32
BF16 = jnp.bfloat16
NZ = 8
BLK = 128
NSLOT = 5
VROW = BLK
DROW = 2 * BLK
BROWS = DROW + 16
NEG = -1e30


def fused_kernel(
    q_hbm, k_hbm, v_hbm, d_hbm, w_ref, out_ref,
    q_ref, k_ref, d_ref, kv, qd, m_sc, acc, den, ring, wv, part, got, fin,
    q_sem, o_sem, wl_sem, c_send, c_recv, k_send, k_recv, y_send, y_recv, n_send, n_recv,
    w_send, w_recv, s_send, s_recv, r_send, r_recv, x_send, x_recv, f_send, f_recv,
):
    pipe, ctx, tp = lax.axis_index("pipe"), lax.axis_index("ctx"), lax.axis_index("tp")
    y_hi, core = pipe // 2, pipe % 2
    y_lo, z = ctx // NZ, ctx % NZ
    o = pipe * 2 + y_lo
    y = y_hi * 2 + y_lo
    n_row = q_hbm.shape[0]
    heads = n_row // BLK
    depth, feats = w_ref.shape

    deep = (y_hi == 1) & (core == 0)
    far_slots = (2, 4)
    feeds = {dlt: (o >= 4 - dlt) & (o <= 5 - dlt) for dlt in (2, 3, 4)}

    def z_dev(direction, reach=1):
        return {"ctx": y_lo * NZ + (z + jnp.where(direction == 0, reach, NZ - reach)) % NZ}

    def o_dev(octet):
        return {"pipe": octet // 2, "ctx": (octet % 2) * NZ + z}

    def y_dev(step):
        to = (y + step) % 4
        return {"pipe": (to // 2) * 2 + core, "ctx": (to % 2) * NZ + z}

    sibling = {"pipe": y_hi * 2 + (1 - core)}
    mate = {"ctx": (1 - y_lo) * NZ + z}

    def signal(barrier, dev):
        pl.semaphore_signal(barrier, inc=1, device_id=dev, device_id_type=MESH)

    own = (
        pltpu.make_async_copy(k_hbm, k_ref, o_sem.at[0]),
        pltpu.make_async_copy(d_hbm, d_ref, o_sem.at[1]),
        pltpu.make_async_copy(v_hbm, kv.at[z, 0, pl.ds(VROW, BLK)], o_sem.at[2]),
    )
    for copy in own:
        copy.start()

    barrier = pltpu.get_barrier_semaphore()
    for dev in (z_dev(0), z_dev(1), z_dev(0, 2), z_dev(1, 2), y_dev(1), y_dev(3), sibling, mate):
        signal(barrier, dev)
    for i in range(1, 4):
        signal(barrier, {"tp": (tp + i) % 4})
    @pl.when(o >= 1)
    def _():
        signal(barrier, o_dev(o - 1))

    @pl.when(deep)
    def _():
        for dlt in (2, 3, 4):
            signal(barrier, o_dev(o - dlt))

    span = BLK // 4 // 2
    seg = span * heads
    half = n_row // 2

    def q_local(t, j):
        return pltpu.make_async_copy(
            q_hbm.at[pl.ds((2 * t + j) * seg, seg)], q_ref.at[pl.ds(j * half + t * seg, seg)],
            q_sem.at[t, j],
        )

    w_local = pltpu.make_async_copy(w_ref, wv.at[0], wl_sem)

    for copy in own:
        copy.wait()
    docs = d_ref[...].astype(F32)
    kv[z, 0, 0:BLK, :] = k_ref[...].T
    kv[z, 0, DROW:BROWS, :] = jnp.broadcast_to(docs, (16, BLK)).astype(BF16)

    asked = jnp.where(o <= 6, 12, 11)
    for dlt in (2, 3, 4):
        asked = asked + jnp.where(feeds[dlt], 1, 0)
    pl.semaphore_wait(barrier, asked)

    def remote(src, dst, send, recv, dev):
        return pltpu.make_async_remote_copy(src, dst, send, recv, device_id=dev, device_id_type=MESH)

    def z_copy(slot, direction, dist):
        src_z = (z + (NZ - 2 if direction == 0 else 2)) % NZ if dist > 2 else z
        rows = pl.ds(0, BROWS)
        if dist == 4:
            rows = pl.ds(0, VROW) if direction == 0 else pl.ds(VROW, BROWS - VROW)
        ref = kv.at[src_z, slot, rows]
        return remote(
            ref, ref, k_send.at[slot, direction, dist - 1], k_recv.at[slot, direction, dist - 1],
            z_dev(direction, 2 - dist % 2),
        )

    def z_send(slot, dists):
        for dist in dists:
            for d in range(2):
                z_copy(slot, d, dist).start()

    def z_wait(slot, dist):
        for d in range(2):
            z_copy(slot, d, dist).wait_recv()

    def col_copy(dlt):
        return remote(
            kv.at[z, 0], kv.at[z, dlt], c_send.at[dlt], c_recv.at[dlt],
            o_dev(jnp.minimum(o + dlt, 7)),
        )

    def y_copy(zz, dlt):
        return remote(
            kv.at[zz, 0], kv.at[zz, dlt], y_send.at[dlt // 2, zz], y_recv.at[dlt // 2, zz],
            o_dev(jnp.minimum(o + dlt, 7)),
        )

    def n_copy(slot, zz):
        return remote(
            kv.at[zz, slot], kv.at[zz, slot + 2], n_send.at[slot, zz], n_recv.at[slot, zz], sibling
        )


    def pass_on(zz):
        @pl.when(o <= 6)
        def _():
            y_copy(zz, 1).start()

        @pl.when(feeds[3])
        def _():
            y_copy(zz, 3).start()

        @pl.when(core == 0)
        def _():
            n_copy(0, zz).start()

    z_send(0, (2, 1))
    for dlt in far_slots:
        @pl.when(feeds[dlt])
        def _(dlt=dlt):
            col_copy(dlt).start()
    pass_on(z)
    for t in range(4):
        for j in range(2):
            q_local(t, j).start()
    w_local.start()

    for dlt in range(1, NSLOT):
        @pl.when(o < dlt)
        def _(dlt=dlt):
            for zz in range(NZ):
                kv[zz, dlt, 0:DROW, :] = jnp.zeros((DROW, BLK), BF16)
                kv[zz, dlt, DROW:BROWS, :] = jnp.full((16, BLK), -1.0, BF16)

    def token_of(row):
        return row % half // seg * (2 * span) + row // half * span + row % seg // heads

    r_i = token_of(lax.broadcasted_iota(jnp.int32, (n_row, BLK), 0))
    c_i = lax.broadcasted_iota(jnp.int32, (n_row, BLK), 1)
    qd[...] = jnp.broadcast_to(
        jnp.sum(jnp.where(r_i == c_i, docs, 0.0), axis=1, keepdims=True), (n_row, BLK)
    )

    def run(fn, lo, hi):
        def body(i, c):
            fn(i)
            return c

        lax.fori_loop(lo, hi, body, 0)

    coef = (BLK ** -0.5) * math.log2(math.e)

    def attend(zz, start, nblk, j, own):
        rb = half

        def body(i):
            rows = pl.ds(pl.multiple_of(i * rb, rb), rb)
            kt = jnp.concatenate([kv[zz, start + b, 0:BLK, :] for b in range(nblk)], axis=1)
            va = jnp.concatenate([kv[zz, start + b, VROW : VROW + BLK, :] for b in range(nblk)], axis=0)
            va = jnp.concatenate([va, jnp.ones((nblk * BLK, BLK), BF16)], axis=1)
            kd = jnp.concatenate(
                [kv[zz, start + b, DROW:BROWS, :][0:1].astype(F32) for b in range(nblk)], axis=1
            )
            s = jnp.dot(q_ref[rows, :], kt, preferred_element_type=F32) * coef
            mask = kd == jnp.concatenate([qd[rows, :]] * nblk, axis=1)
            if own:
                ri = token_of(lax.broadcasted_iota(jnp.int32, (rb, nblk * BLK), 0) + i * rb)
                ci = lax.broadcasted_iota(jnp.int32, (rb, nblk * BLK), 1)
                mask = mask & ((ci <= ri) | (ci >= BLK))
            s = jnp.where(mask, s, NEG)
            top = jnp.max(s, axis=1, keepdims=True)
            if own:
                m_new = jnp.broadcast_to(top, (rb, BLK))
            else:
                m_old = m_sc[rows, :]
                m_new = jnp.maximum(m_old, top)
            p = jnp.exp2(s - jnp.concatenate([m_new] * nblk, axis=1)).astype(BF16)
            res = jnp.dot(p, va, preferred_element_type=F32)
            if own:
                acc[rows, :] = res[:, :BLK]
                den[rows, :] = res[:, BLK:]
            else:
                alpha = jnp.exp2(m_old - m_new)
                acc[rows, :] = acc[rows, :] * alpha + res[:, :BLK]
                den[rows, :] = den[rows, :] * alpha + res[:, BLK:]
            m_sc[rows, :] = m_new

        body(j)

    def sides(*spots):
        for zz in spots:
            @pl.when(o >= 1)
            def _(zz=zz):
                y_copy(zz, 1).wait_recv()

                @pl.when(core == 0)
                def _():
                    n_copy(1, zz).start()

            @pl.when(deep)
            def _(zz=zz):
                y_copy(zz, 3).wait_recv()

        for zz in spots:
            for slot in range(3):
                @pl.when((core == 1) & (o - 2 >= slot))
                def _(slot=slot, zz=zz):
                    n_copy(slot, zz).wait_recv()

    quarter_w = depth // 4

    def w_copy(i):
        rows = pl.ds((2 * i + core) * quarter_w, quarter_w)
        return remote(w_ref.at[rows], wv.at[1, rows], w_send.at[i], w_recv.at[i], y_dev(1 + 2 * i))

    def s_copy(i):
        rows = pl.ds((2 * i + core) * quarter_w, quarter_w)
        return remote(wv.at[1, rows], wv.at[1, rows], s_send.at[i], s_recv.at[i], sibling)

    def around(dist):
        return (z + NZ - dist) % NZ, (z + dist) % NZ

    @pl.when(deep)
    def _():
        for dlt in far_slots:
            col_copy(dlt).wait_recv()
            z_send(dlt, (2, 1))
            if dlt == 2:
                n_copy(2, z).start()

    z_wait(0, 2)
    z_send(0, (3, 4))
    for dist in (2, 1):
        if dist == 1:
            z_wait(0, 1)
        for zz in around(dist):
            pass_on(zz)

    for t in range(4):
        for j in range(2):
            q_local(t, j).wait()
    sides(z)
    run(lambda j: attend(z, 0, NSLOT, j, True), 0, 2)

    def far_wait(dist):
        @pl.when(deep)
        def _():
            for slot in far_slots:
                z_wait(slot, dist)
                if dist == 2:
                    z_send(slot, (3, 4))
                if slot == 2:
                    for zz in around(dist)[: 1 if dist == 4 else 2]:
                        n_copy(2, zz).start()

    def arrivals(dist, carry):
        @pl.when(dist == 1)
        def _():
            z_wait(0, 3)
            for zz in around(3):
                pass_on(zz)
            far_wait(2)
            far_wait(1)
            sides(*around(1))

        @pl.when(dist == 2)
        def _():
            z_wait(0, 4)
            pass_on((z + 4) % NZ)
            sides(*around(2))

        @pl.when(dist == 3)
        def _():
            far_wait(3)
            far_wait(4)
            for j in range(2):
                w_copy(j).start()
            sides(*around(3))

        both = dist < 3
        side = jnp.where(both, 2, 1)
        run(
            lambda i: early(
                (z + jnp.where(i < side, NZ - dist, dist)) % NZ, jnp.where(both, i % 2, 0)
            ),
            0, 2 * side,
        )
        return carry

    def early(zz, j):
        attend(zz, jnp.where(zz < z, 0, 1), NSLOT - 1, j, False)

    lax.fori_loop(1, 4, arrivals, 0)
    sides((z + 4) % NZ)

    def r_copy(direction, hop, j):
        src_z = (z + jnp.where(direction == 0, NZ + 1 - hop, hop - 1)) % NZ
        ref = ring.at[src_z, j]
        return remote(
            ref, ref, r_send.at[direction, hop - 1, j], r_recv.at[direction, hop - 1, j],
            z_dev(direction),
        )

    def finish(j):
        run(lambda i: early((z + i) % NZ, j), jnp.where(j == 0, 4, 3), jnp.where(j == 0, 5, 6))
        for h in range(heads):
            rows = pl.ds(j * half + h, BLK // 2, stride=heads)
            ring[z, j, :, h * BLK : (h + 1) * BLK] = (acc[rows, :] / den[rows, :]).astype(BF16)
        for direction in range(2):
            r_copy(direction, 1, j).start()

    run(finish, 0, 2)

    def x_copy(s, wh, i):
        to = (tp + i) % 4
        return remote(
            part.at[s, wh, to], got.at[s, wh, i - 1],
            x_send.at[s, wh, i - 1], x_recv.at[s, wh, i - 1], {"tp": to},
        )

    def where_of(s):
        hop, j = (s + 1) // 2, (s + 1) % 2
        end = (s == 0) | (s == 7)
        za = (z + jnp.where(s == 0, 0, jnp.where(s == 7, 4, NZ - hop))) % NZ
        zb = (z + jnp.where(s == 0, 0, jnp.where(s == 7, 4, hop))) % NZ
        return (za, jnp.where(end, 0, j)), (zb, jnp.where(end, 1, j))

    def f_copy(s, side, spot):
        zz, j = spot
        return remote(
            fin.at[s, pl.ds(side * span, span)],
            out_ref.at[y_lo * NZ + zz, pl.ds(pl.multiple_of(j * span, span), span)],
            f_send.at[s, side], f_recv.at[s, side], mate,
        )

    NT = 256

    def multiply(s, wh):
        (za, ja), (zb, jb) = where_of(s)

        def cols(n, c):
            lanes = pl.ds(pl.multiple_of(n * NT, NT), NT)
            x = jnp.concatenate([ring[za, ja], ring[zb, jb]], axis=0)
            res = jnp.dot(x, wv[wh, :, lanes], preferred_element_type=F32).astype(BF16)
            for side in range(2):
                for t in range(4):
                    part[s, wh, t, side * span : (side + 1) * span, lanes] = res[
                        (side * 4 + t) * span : (side * 4 + t + 1) * span
                    ]
            return c

        lax.fori_loop(0, feats // NT, cols, 0)
        for i in range(1, 4):
            x_copy(s, wh, i).start()

    def reduce(s):
        sums = []
        for wh in (1, 0):
            for i in range(1, 4):
                x_copy(s, wh, i).wait_recv()
            total = part[s, wh, tp].astype(F32)
            for i in range(3):
                total = total + got[s, wh, i].astype(F32)
            total = total.astype(BF16)
            for side, spot in enumerate(where_of(s)):
                if wh == 1:
                    if side == 0:
                        fin[s] = total
                    f_copy(s, side, spot).start()
                else:
                    out_ref[y_lo * NZ + spot[0], pl.ds(pl.multiple_of(spot[1] * span, span), span), :] = total[
                        side * span : (side + 1) * span
                    ]

    w_local.wait()
    multiply(0, 0)

    LATE = 3

    def steps(s, carry):
        hop, j = (s + 1) // 2, (s + 1) % 2
        for direction in range(2):
            r_copy(direction, hop, j).wait_recv()

            @pl.when((hop < 3) | (j == direction))
            def _(direction=direction):
                r_copy(direction, hop + 1, j).start()

        @pl.when(s == LATE - 1)
        def _():
            for i in range(2):
                w_copy(i).wait_recv()
                s_copy(i).start()

        @pl.when(s == LATE)
        def _():
            for i in range(2):
                s_copy(i).wait_recv()

        first = jnp.where(s < LATE, s, jnp.where(s == LATE, 0, s))
        run(lambda i: multiply(jnp.where(i == 0, s, first + i - 1), jnp.where(i == 0, 0, 1)), 0,
            jnp.where(s < LATE, 1, s - first + 2))
        run(reduce, jnp.where(s == LATE + 1, 0, s - 2), jnp.where(s <= LATE, s - 2, s - 1))
        return carry

    lax.fori_loop(1, 7, steps, 0)
    for d in range(2):
        r_copy(d, 4, d).wait_recv()
    run(lambda i: multiply(7, 1 - i), 0, 2)
    run(reduce, 5, 8)

    def drain(s, c):
        for wh in range(2):
            for i in range(1, 4):
                x_copy(s, wh, i).wait_send()
        for side, spot in enumerate(where_of(s)):
            f_copy(s, side, spot).wait()

        @pl.when(o <= 6)
        def _():
            y_copy(s, 1).wait_send()

        @pl.when(feeds[3])
        def _():
            y_copy(s, 3).wait_send()

        for slot in range(3):
            @pl.when((core == 0) & (o >= slot))
            def _(slot=slot):
                n_copy(slot, s).wait_send()

        return c

    lax.fori_loop(0, NZ, drain, 0)
    for direction in range(2):
        for hop in range(1, 5):
            for j in range(2):
                if hop < 4 or j == direction:
                    r_copy(direction, hop, j).wait_send()
            z_copy(0, direction, hop).wait_send()

            @pl.when(deep)
            def _(direction=direction, hop=hop):
                for slot in far_slots:
                    z_copy(slot, direction, hop).wait_send()
    for dlt in far_slots:
        @pl.when(feeds[dlt])
        def _(dlt=dlt):
            col_copy(dlt).wait_send()
    for i in range(2):
        w_copy(i).wait_send()
        s_copy(i).wait_send()


def fused(q, k, v, docs, w):
    n_row = q.shape[0]
    depth, feats = w.shape
    quarter = BLK // 4
    dma = pltpu.SemaphoreType.DMA
    vmem = pl.BlockSpec(memory_space=pltpu.VMEM)
    return pl.pallas_call(
        fused_kernel,
        name="attend_project",
        out_shape=jax.ShapeDtypeStruct((2 * NZ, quarter, feats), BF16),
        in_specs=[pl.BlockSpec(memory_space=pl.ANY)] * 5,
        out_specs=vmem,
        scratch_shapes=[
            pltpu.VMEM((n_row, BLK), BF16),
            pltpu.VMEM((BLK, BLK), BF16),
            pltpu.VMEM((1, BLK), jnp.int32),
            pltpu.VMEM((NZ, NSLOT, BROWS, BLK), BF16),
            pltpu.VMEM((n_row, BLK), F32),
            pltpu.VMEM((n_row, BLK), F32),
            pltpu.VMEM((n_row, BLK), F32),
            pltpu.VMEM((n_row, BLK), F32),
            pltpu.VMEM((NZ, 2, BLK // 2, depth), BF16),
            pltpu.VMEM((2, depth, feats), BF16),
            pltpu.VMEM((NZ, 2, 4, quarter, feats), BF16),
            pltpu.VMEM((NZ, 2, 3, quarter, feats), BF16),
            pltpu.VMEM((NZ, quarter, feats), BF16),
            dma((4, 2)),
            dma((3,)),
            dma,
            dma((NSLOT,)),
            dma((NSLOT,)),
            dma((NSLOT, 2, 4)),
            dma((NSLOT, 2, 4)),
            dma((2, NZ)),
            dma((2, NZ)),
            dma((3, NZ)),
            dma((3, NZ)),
            dma((2,)),
            dma((2,)),
            dma((2,)),
            dma((2,)),
            dma((2, 4, 2)),
            dma((2, 4, 2)),
            dma((NZ, 2, 3)),
            dma((NZ, 2, 3)),
            dma((NZ, 2)),
            dma((NZ, 2)),
        ],
        compiler_params=pltpu.CompilerParams(
            collective_id=0, has_side_effects=True, vmem_limit_bytes=60 * 2**20
        ),
    )(q, k, v, docs, w)


def shards(query_rows, key_rows, value_rows, doc_ids, out_weight):
    tokens, heads, width = query_rows.shape
    q = query_rows.reshape(tokens * heads, width)
    k = key_rows.reshape(tokens, width)
    v = value_rows.reshape(tokens, width)
    out = fused(q, k, v, doc_ids.reshape(1, tokens), out_weight)
    return out.reshape(1, 2 * NZ, 1, tokens // 4, out_weight.shape[1])


def solution(mesh):
    return jax.shard_map(
        shards,
        mesh=mesh,
        in_specs=(
            P(("pipe", "ctx"), "tp", None),
            P(("pipe", "ctx"), "tp", None),
            P(("pipe", "ctx"), "tp", None),
            P(("pipe", "ctx")),
            P("tp", "ctx"),
        ),
        out_specs=P("pipe", None, "tp", None, "ctx"),
        check_vma=False,
    )
```

```python
import math

import jax
import jax.numpy as jnp
from jax import lax
from jax.experimental import pallas as pl
from jax.experimental.pallas import tpu as pltpu
from jax.sharding import PartitionSpec as P

MESH = pl.DeviceIdType.MESH
F32 = jnp.float32
BF16 = jnp.bfloat16
NZ = 8
BLK = 128
NSLOT = 5
VROW = BLK
DROW = 2 * BLK
BROWS = DROW + 16
NEG = -1e30


def fused_kernel(
    q_hbm, k_hbm, v_hbm, d_hbm, w_ref, out_ref,
    q_ref, k_ref, d_ref, kv, qd, m_sc, acc, den, ring, wv, part, got, fin,
    q_sem, o_sem, wl_sem, c_send, c_recv, k_send, k_recv, y_send, y_recv, n_send, n_recv,
    w_send, w_recv, s_send, s_recv, r_send, r_recv, x_send, x_recv, f_send, f_recv,
):
    pipe, ctx, tp = lax.axis_index("pipe"), lax.axis_index("ctx"), lax.axis_index("tp")
    y_hi, core = pipe // 2, pipe % 2
    y_lo, z = ctx // NZ, ctx % NZ
    o = pipe * 2 + y_lo
    y = y_hi * 2 + y_lo
    n_row = q_hbm.shape[0]
    heads = n_row // BLK
    depth, feats = w_ref.shape

    deep = (y_hi == 1) & (core == 0)
    far_slots = (2, 4)
    feeds = {dlt: (o >= 4 - dlt) & (o <= 5 - dlt) for dlt in (2, 3, 4)}

    def z_dev(direction, reach=1):
        return {"ctx": y_lo * NZ + (z + jnp.where(direction == 0, reach, NZ - reach)) % NZ}

    def o_dev(octet):
        return {"pipe": octet // 2, "ctx": (octet % 2) * NZ + z}

    def y_dev(step):
        to = (y + step) % 4
        return {"pipe": (to // 2) * 2 + core, "ctx": (to % 2) * NZ + z}

    sibling = {"pipe": y_hi * 2 + (1 - core)}
    mate = {"ctx": (1 - y_lo) * NZ + z}

    def signal(barrier, dev):
        pl.semaphore_signal(barrier, inc=1, device_id=dev, device_id_type=MESH)

    own = (
        pltpu.make_async_copy(k_hbm, k_ref, o_sem.at[0]),
        pltpu.make_async_copy(d_hbm, d_ref, o_sem.at[1]),
        pltpu.make_async_copy(v_hbm, kv.at[z, 0, pl.ds(VROW, BLK)], o_sem.at[2]),
    )
    for copy in own:
        copy.start()

    barrier = pltpu.get_barrier_semaphore()
    for dev in (z_dev(0), z_dev(1), z_dev(0, 2), z_dev(1, 2), y_dev(1), y_dev(3), sibling, mate):
        signal(barrier, dev)
    for i in range(1, 4):
        signal(barrier, {"tp": (tp + i) % 4})
    @pl.when(o >= 1)
    def _():
        signal(barrier, o_dev(o - 1))

    @pl.when(deep)
    def _():
        for dlt in (2, 3, 4):
            signal(barrier, o_dev(o - dlt))

    span = BLK // 4 // 2
    seg = span * heads
    half = n_row // 2

    def q_local(t, j):
        return pltpu.make_async_copy(
            q_hbm.at[pl.ds((2 * t + j) * seg, seg)], q_ref.at[pl.ds(j * half + t * seg, seg)],
            q_sem.at[t, j],
        )

    w_local = pltpu.make_async_copy(w_ref, wv.at[0], wl_sem)

    for copy in own:
        copy.wait()
    docs = d_ref[...].astype(F32)
    kv[z, 0, 0:BLK, :] = k_ref[...].T
    kv[z, 0, DROW:BROWS, :] = jnp.broadcast_to(docs, (16, BLK)).astype(BF16)

    asked = jnp.where(o <= 6, 12, 11)
    for dlt in (2, 3, 4):
        asked = asked + jnp.where(feeds[dlt], 1, 0)
    pl.semaphore_wait(barrier, asked)

    def remote(src, dst, send, recv, dev):
        return pltpu.make_async_remote_copy(src, dst, send, recv, device_id=dev, device_id_type=MESH)

    def z_copy(slot, direction, dist):
        src_z = (z + (NZ - 2 if direction == 0 else 2)) % NZ if dist > 2 else z
        rows = pl.ds(0, BROWS)
        if dist == 4:
            rows = pl.ds(0, VROW) if direction == 0 else pl.ds(VROW, BROWS - VROW)
        ref = kv.at[src_z, slot, rows]
        return remote(
            ref, ref, k_send.at[slot, direction, dist - 1], k_recv.at[slot, direction, dist - 1],
            z_dev(direction, 2 - dist % 2),
        )

    def z_send(slot, dists):
        for dist in dists:
            for d in range(2):
                z_copy(slot, d, dist).start()

    def z_wait(slot, dist):
        for d in range(2):
            z_copy(slot, d, dist).wait_recv()

    def col_copy(dlt):
        return remote(
            kv.at[z, 0], kv.at[z, dlt], c_send.at[dlt], c_recv.at[dlt],
            o_dev(jnp.minimum(o + dlt, 7)),
        )

    def y_copy(zz, dlt):
        return remote(
            kv.at[zz, 0], kv.at[zz, dlt], y_send.at[dlt // 2, zz], y_recv.at[dlt // 2, zz],
            o_dev(jnp.minimum(o + dlt, 7)),
        )

    def n_copy(slot, zz):
        return remote(
            kv.at[zz, slot], kv.at[zz, slot + 2], n_send.at[slot, zz], n_recv.at[slot, zz], sibling
        )


    def pass_on(zz):
        @pl.when(o <= 6)
        def _():
            y_copy(zz, 1).start()

        @pl.when(feeds[3])
        def _():
            y_copy(zz, 3).start()

        @pl.when(core == 0)
        def _():
            n_copy(0, zz).start()

    z_send(0, (2, 1))
    for dlt in far_slots:
        @pl.when(feeds[dlt])
        def _(dlt=dlt):
            col_copy(dlt).start()
    pass_on(z)
    for t in range(4):
        for j in range(2):
            q_local(t, j).start()
    w_local.start()

    for dlt in range(1, NSLOT):
        @pl.when(o < dlt)
        def _(dlt=dlt):
            for zz in range(NZ):
                kv[zz, dlt, 0:DROW, :] = jnp.zeros((DROW, BLK), BF16)
                kv[zz, dlt, DROW:BROWS, :] = jnp.full((16, BLK), -1.0, BF16)

    def token_of(row):
        return row % half // seg * (2 * span) + row // half * span + row % seg // heads

    r_i = token_of(lax.broadcasted_iota(jnp.int32, (n_row, BLK), 0))
    c_i = lax.broadcasted_iota(jnp.int32, (n_row, BLK), 1)
    qd[...] = jnp.broadcast_to(
        jnp.sum(jnp.where(r_i == c_i, docs, 0.0), axis=1, keepdims=True), (n_row, BLK)
    )

    def run(fn, lo, hi):
        def body(i, c):
            fn(i)
            return c

        lax.fori_loop(lo, hi, body, 0)

    coef = (BLK ** -0.5) * math.log2(math.e)

    def attend(zz, start, nblk, j, own):
        rb = half

        def body(i):
            rows = pl.ds(pl.multiple_of(i * rb, rb), rb)
            kt = jnp.concatenate([kv[zz, start + b, 0:BLK, :] for b in range(nblk)], axis=1)
            va = jnp.concatenate([kv[zz, start + b, VROW : VROW + BLK, :] for b in range(nblk)], axis=0)
            va = jnp.concatenate([va, jnp.ones((nblk * BLK, BLK), BF16)], axis=1)
            kd = jnp.concatenate(
                [kv[zz, start + b, DROW:BROWS, :][0:1].astype(F32) for b in range(nblk)], axis=1
            )
            s = jnp.dot(q_ref[rows, :], kt, preferred_element_type=F32) * coef
            mask = kd == jnp.concatenate([qd[rows, :]] * nblk, axis=1)
            if own:
                ri = token_of(lax.broadcasted_iota(jnp.int32, (rb, nblk * BLK), 0) + i * rb)
                ci = lax.broadcasted_iota(jnp.int32, (rb, nblk * BLK), 1)
                mask = mask & ((ci <= ri) | (ci >= BLK))
            s = jnp.where(mask, s, NEG)
            top = jnp.max(s, axis=1, keepdims=True)
            if own:
                m_new = jnp.broadcast_to(top, (rb, BLK))
            else:
                m_old = m_sc[rows, :]
                m_new = jnp.maximum(m_old, top)
            p = jnp.exp2(s - jnp.concatenate([m_new] * nblk, axis=1)).astype(BF16)
            res = jnp.dot(p, va, preferred_element_type=F32)
            if own:
                acc[rows, :] = res[:, :BLK]
                den[rows, :] = res[:, BLK:]
            else:
                alpha = jnp.exp2(m_old - m_new)
                acc[rows, :] = acc[rows, :] * alpha + res[:, :BLK]
                den[rows, :] = den[rows, :] * alpha + res[:, BLK:]
            m_sc[rows, :] = m_new

        body(j)

    def sides(*spots):
        for zz in spots:
            @pl.when(o >= 1)
            def _(zz=zz):
                y_copy(zz, 1).wait_recv()

                @pl.when(core == 0)
                def _():
                    n_copy(1, zz).start()

            @pl.when(deep)
            def _(zz=zz):
                y_copy(zz, 3).wait_recv()

        for zz in spots:
            for slot in range(3):
                @pl.when((core == 1) & (o - 2 >= slot))
                def _(slot=slot, zz=zz):
                    n_copy(slot, zz).wait_recv()

    quarter_w = depth // 4

    def w_copy(i):
        rows = pl.ds((2 * i + core) * quarter_w, quarter_w)
        return remote(w_ref.at[rows], wv.at[1, rows], w_send.at[i], w_recv.at[i], y_dev(1 + 2 * i))

    def s_copy(i):
        rows = pl.ds((2 * i + core) * quarter_w, quarter_w)
        return remote(wv.at[1, rows], wv.at[1, rows], s_send.at[i], s_recv.at[i], sibling)

    def around(dist):
        return (z + NZ - dist) % NZ, (z + dist) % NZ

    @pl.when(deep)
    def _():
        for dlt in far_slots:
            col_copy(dlt).wait_recv()
            z_send(dlt, (2, 1))
            if dlt == 2:
                n_copy(2, z).start()

    z_wait(0, 2)
    z_send(0, (3, 4))
    for dist in (2, 1):
        if dist == 1:
            z_wait(0, 1)
        for zz in around(dist):
            pass_on(zz)

    for t in range(4):
        for j in range(2):
            q_local(t, j).wait()
    sides(z)
    run(lambda j: attend(z, 0, NSLOT, j, True), 0, 2)

    def far_wait(dist):
        @pl.when(deep)
        def _():
            for slot in far_slots:
                z_wait(slot, dist)
                if dist == 2:
                    z_send(slot, (3, 4))
                if slot == 2:
                    for zz in around(dist)[: 1 if dist == 4 else 2]:
                        n_copy(2, zz).start()

    def arrivals(dist, carry):
        @pl.when(dist == 1)
        def _():
            far_wait(2)
            z_wait(0, 3)
            for zz in around(3):
                pass_on(zz)
            far_wait(1)
            sides(*around(1))

        @pl.when(dist == 2)
        def _():
            z_wait(0, 4)
            pass_on((z + 4) % NZ)
            sides(*around(2))

        @pl.when(dist == 3)
        def _():
            far_wait(3)
            far_wait(4)
            for j in range(2):
                w_copy(j).start()
            sides(*around(3))

        both = dist < 3
        side = jnp.where(both, 2, 1)
        run(
            lambda i: early(
                (z + jnp.where(i < side, NZ - dist, dist)) % NZ, jnp.where(both, i % 2, 0)
            ),
            0, 2 * side,
        )
        return carry

    def early(zz, j):
        attend(zz, jnp.where(zz < z, 0, 1), NSLOT - 1, j, False)

    lax.fori_loop(1, 4, arrivals, 0)
    sides((z + 4) % NZ)

    def r_copy(direction, hop, j):
        src_z = (z + jnp.where(direction == 0, NZ + 1 - hop, hop - 1)) % NZ
        ref = ring.at[src_z, j]
        return remote(
            ref, ref, r_send.at[direction, hop - 1, j], r_recv.at[direction, hop - 1, j],
            z_dev(direction),
        )

    def finish(j):
        run(lambda i: early((z + i) % NZ, j), jnp.where(j == 0, 4, 3), jnp.where(j == 0, 5, 6))
        for h in range(heads):
            rows = pl.ds(j * half + h, BLK // 2, stride=heads)
            ring[z, j, :, h * BLK : (h + 1) * BLK] = (acc[rows, :] / den[rows, :]).astype(BF16)
        for direction in range(2):
            r_copy(direction, 1, j).start()

    run(finish, 0, 2)

    def x_copy(s, wh, i):
        to = (tp + i) % 4
        return remote(
            part.at[s, wh, to], got.at[s, wh, i - 1],
            x_send.at[s, wh, i - 1], x_recv.at[s, wh, i - 1], {"tp": to},
        )

    def where_of(s):
        hop, j = (s + 1) // 2, (s + 1) % 2
        end = (s == 0) | (s == 7)
        za = (z + jnp.where(s == 0, 0, jnp.where(s == 7, 4, NZ - hop))) % NZ
        zb = (z + jnp.where(s == 0, 0, jnp.where(s == 7, 4, hop))) % NZ
        return (za, jnp.where(end, 0, j)), (zb, jnp.where(end, 1, j))

    def f_copy(s, side, spot):
        zz, j = spot
        return remote(
            fin.at[s, pl.ds(side * span, span)],
            out_ref.at[y_lo * NZ + zz, pl.ds(pl.multiple_of(j * span, span), span)],
            f_send.at[s, side], f_recv.at[s, side], mate,
        )

    NT = 256

    def multiply(s, wh):
        (za, ja), (zb, jb) = where_of(s)

        def cols(n, c):
            lanes = pl.ds(pl.multiple_of(n * NT, NT), NT)
            x = jnp.concatenate([ring[za, ja], ring[zb, jb]], axis=0)
            res = jnp.dot(x, wv[wh, :, lanes], preferred_element_type=F32).astype(BF16)
            for side in range(2):
                for t in range(4):
                    part[s, wh, t, side * span : (side + 1) * span, lanes] = res[
                        (side * 4 + t) * span : (side * 4 + t + 1) * span
                    ]
            return c

        lax.fori_loop(0, feats // NT, cols, 0)
        for i in range(1, 4):
            x_copy(s, wh, i).start()

    def reduce(s):
        sums = []
        for wh in (1, 0):
            for i in range(1, 4):
                x_copy(s, wh, i).wait_recv()
            total = part[s, wh, tp].astype(F32)
            for i in range(3):
                total = total + got[s, wh, i].astype(F32)
            total = total.astype(BF16)
            for side, spot in enumerate(where_of(s)):
                if wh == 1:
                    if side == 0:
                        fin[s] = total
                    f_copy(s, side, spot).start()
                else:
                    out_ref[y_lo * NZ + spot[0], pl.ds(pl.multiple_of(spot[1] * span, span), span), :] = total[
                        side * span : (side + 1) * span
                    ]

    w_local.wait()
    multiply(0, 0)

    LATE = 3

    def steps(s, carry):
        hop, j = (s + 1) // 2, (s + 1) % 2
        for direction in range(2):
            r_copy(direction, hop, j).wait_recv()

            @pl.when((hop < 3) | (j == direction))
            def _(direction=direction):
                r_copy(direction, hop + 1, j).start()

        @pl.when(s == LATE - 1)
        def _():
            for i in range(2):
                w_copy(i).wait_recv()
                s_copy(i).start()

        @pl.when(s == LATE)
        def _():
            for i in range(2):
                s_copy(i).wait_recv()

        first = jnp.where(s < LATE, s, jnp.where(s == LATE, 0, s))
        run(lambda i: multiply(jnp.where(i == 0, s, first + i - 1), jnp.where(i == 0, 0, 1)), 0,
            jnp.where(s < LATE, 1, s - first + 2))
        run(reduce, jnp.where(s == LATE + 1, 0, s - 2), jnp.where(s <= LATE, s - 2, s - 1))
        return carry

    lax.fori_loop(1, 7, steps, 0)
    for d in range(2):
        r_copy(d, 4, d).wait_recv()
    run(lambda i: multiply(7, 1 - i), 0, 2)
    run(reduce, 5, 8)

    def drain(s, c):
        for wh in range(2):
            for i in range(1, 4):
                x_copy(s, wh, i).wait_send()
        for side, spot in enumerate(where_of(s)):
            f_copy(s, side, spot).wait()

        @pl.when(o <= 6)
        def _():
            y_copy(s, 1).wait_send()

        @pl.when(feeds[3])
        def _():
            y_copy(s, 3).wait_send()

        for slot in range(3):
            @pl.when((core == 0) & (o >= slot))
            def _(slot=slot):
                n_copy(slot, s).wait_send()

        return c

    lax.fori_loop(0, NZ, drain, 0)
    for direction in range(2):
        for hop in range(1, 5):
            for j in range(2):
                if hop < 4 or j == direction:
                    r_copy(direction, hop, j).wait_send()
            z_copy(0, direction, hop).wait_send()

            @pl.when(deep)
            def _(direction=direction, hop=hop):
                for slot in far_slots:
                    z_copy(slot, direction, hop).wait_send()
    for dlt in far_slots:
        @pl.when(feeds[dlt])
        def _(dlt=dlt):
            col_copy(dlt).wait_send()
    for i in range(2):
        w_copy(i).wait_send()
        s_copy(i).wait_send()


def fused(q, k, v, docs, w):
    n_row = q.shape[0]
    depth, feats = w.shape
    quarter = BLK // 4
    dma = pltpu.SemaphoreType.DMA
    vmem = pl.BlockSpec(memory_space=pltpu.VMEM)
    return pl.pallas_call(
        fused_kernel,
        name="attend_project",
        out_shape=jax.ShapeDtypeStruct((2 * NZ, quarter, feats), BF16),
        in_specs=[pl.BlockSpec(memory_space=pltpu.HBM)] * 5,
        out_specs=vmem,
        scratch_shapes=[
            pltpu.VMEM((n_row, BLK), BF16),
            pltpu.VMEM((BLK, BLK), BF16),
            pltpu.VMEM((1, BLK), jnp.int32),
            pltpu.VMEM((NZ, NSLOT, BROWS, BLK), BF16),
            pltpu.VMEM((n_row, BLK), F32),
            pltpu.VMEM((n_row, BLK), F32),
            pltpu.VMEM((n_row, BLK), F32),
            pltpu.VMEM((n_row, BLK), F32),
            pltpu.VMEM((NZ, 2, BLK // 2, depth), BF16),
            pltpu.VMEM((2, depth, feats), BF16),
            pltpu.VMEM((NZ, 2, 4, quarter, feats), BF16),
            pltpu.VMEM((NZ, 2, 3, quarter, feats), BF16),
            pltpu.VMEM((NZ, quarter, feats), BF16),
            dma((4, 2)),
            dma((3,)),
            dma,
            dma((NSLOT,)),
            dma((NSLOT,)),
            dma((NSLOT, 2, 4)),
            dma((NSLOT, 2, 4)),
            dma((2, NZ)),
            dma((2, NZ)),
            dma((3, NZ)),
            dma((3, NZ)),
            dma((2,)),
            dma((2,)),
            dma((2,)),
            dma((2,)),
            dma((2, 4, 2)),
            dma((2, 4, 2)),
            dma((NZ, 2, 3)),
            dma((NZ, 2, 3)),
            dma((NZ, 2)),
            dma((NZ, 2)),
        ],
        compiler_params=pltpu.CompilerParams(
            collective_id=0, has_side_effects=True, vmem_limit_bytes=48 * 2**20
        ),
    )(*[pltpu.with_memory_space_constraint(x, pltpu.HBM) for x in (q, k, v, docs, w)])


def shards(query_rows, key_rows, value_rows, doc_ids, out_weight):
    tokens, heads, width = query_rows.shape
    q = query_rows.reshape(tokens * heads, width)
    k = key_rows.reshape(tokens, width)
    v = value_rows.reshape(tokens, width)
    out = fused(q, k, v, doc_ids.reshape(1, tokens), out_weight)
    return out.reshape(1, 2 * NZ, 1, tokens // 4, out_weight.shape[1])


def solution(mesh):
    return jax.shard_map(
        shards,
        mesh=mesh,
        in_specs=(
            P(("pipe", "ctx"), "tp", None),
            P(("pipe", "ctx"), "tp", None),
            P(("pipe", "ctx"), "tp", None),
            P(("pipe", "ctx")),
            P("tp", "ctx"),
        ),
        out_specs=P("pipe", None, "tp", None, "ctx"),
        check_vma=False,
    )
```
